128 devices in a mesh: seq: 16 (over x, y_hi, core), fsdp: 8 (over z, y_lo).
Axes of the slice: x: 4, y: 4 (y_hi: 2, y_lo: 2; y = y_hi * 2 + y_lo), z: 4, core: 2. Of those that a mesh axis runs over, the one named last changes fastest.
Arguments:
- normed: bfloat16 [131072, 1024], P(('seq', 'fsdp')), may hold values from -31 to 31, as said below
- w_qkv: bfloat16 [1024, 3072], P('fsdp'), may hold values from -0.5 to 0.5, as said below
- w_out: bfloat16 [1024, 1024], P('fsdp'), may hold values from -0.5 to 0.5
- layout: int32 [1024, 10], P(('seq', 'fsdp')), may hold values from 0 to 23, as said below
- counts: int32 [1024], P(('seq', 'fsdp')), may hold values from 1 to 10, as said below
Outputs:
- mixed: bfloat16 [131072, 1024], P(('seq', 'fsdp'))
The draws below stay inside these ranges and needn't reach their ends.
Inputs may be any that keep to these rules, and one draw needn't show every extreme that they name: `normed`: float activations. `w_qkv`: float weights. `layout`: each row holds 10 distinct pool entries, never the query block's own entry; entries 0 to 7 name the blocks of the station one step lower along seq, the last 8 those one step higher. `counts`: the value 10 occurs in every draw.
All inputs are finite; a program needn't handle non-finite values.
Results may differ from the reference program's by a relative error of at most 0.0099.
Values may be sent and summed in bfloat16 or wider, within the bound.
A program may use at most 128 MiB of HBM per device.

```python
import math
import jax
import jax.numpy as jnp
from jax import lax

D = 1024
HEADS = 8
BLOCK = 128
KEY_BLOCKS = 10
ROWS_DEV = 1024
TOKENS = 131072
QUERY_BLOCKS = 1024
N_SEQ = 16
N_FSDP = 8


def draw_normed(key, part):
    base = jax.random.truncated_normal(key, -6.0, 6.0, (TOKENS, D), jnp.float32)
    return base.astype(jnp.bfloat16)


def draw_w_qkv(key, part):
    first_key = jax.random.fold_in(jax.random.fold_in(key, 11), 0)
    base = jax.random.truncated_normal(first_key, -6.0, 6.0, (D, 3 * D), jnp.float32) / math.sqrt(D)
    query_cols = base[:, :D] * 1.7
    key_cols = base[:, D:2 * D] * 1.7
    value_cols = base[:, 2 * D:]
    joined = jnp.concatenate([query_cols, key_cols, value_cols], axis=1)
    return jnp.clip(joined, -0.5, 0.5).astype(jnp.bfloat16)


def draw_layout(key, part):
    blocks_here = ROWS_DEV // BLOCK
    pool_size = 3 * blocks_here
    raw = jax.random.randint(jax.random.fold_in(key, 23), (QUERY_BLOCKS, pool_size), 0, 1 << 20)
    column = jnp.arange(pool_size, dtype=jnp.int32)
    distinct = raw * pool_size + column[None, :]
    own_entry = blocks_here + jnp.arange(QUERY_BLOCKS, dtype=jnp.int32) % blocks_here
    distinct = jnp.where(column[None, :] == own_entry[:, None], jnp.int32(1 << 30), distinct)
    order = jnp.argsort(distinct, axis=1, stable=True)
    return order[:, :KEY_BLOCKS].astype(jnp.int32)


def draw_counts(key, part):
    drawn = jax.random.randint(jax.random.fold_in(key, 31), (QUERY_BLOCKS,), 1, KEY_BLOCKS + 1)
    first = jnp.arange(QUERY_BLOCKS, dtype=jnp.int32) == 0
    return jnp.where(first, jnp.int32(KEY_BLOCKS), drawn).astype(jnp.int32)


def levels(key, dims, cuts, least, top_value):
    gain = 1.0
    for dim, parts in cuts:
        draws = jax.random.uniform(jax.random.fold_in(jax.random.fold_in(key, 6), dim), (parts,), jnp.float32, least / len(cuts), top_value / len(cuts))
        gain = gain * jnp.repeat(jnp.exp(draws), dims[dim] // parts).reshape((-1,) + (1,) * (len(dims) - 1 - dim))
    return gain


def scatter_about(stream_key, dims, width, bound, cuts=(), held_as=jnp.bfloat16):
    array = width * jax.random.normal(stream_key, dims, jnp.float32)
    if cuts:
        array = array * levels(stream_key, dims, cuts, -0.22, 0.18)
    return jnp.clip(array, -bound, bound).astype(held_as)


def setup_inputs(seed: int = 0) -> dict:
    keys = jax.random.split(jax.random.key(seed), 6)
    return {
        "normed": draw_normed(jax.random.fold_in(keys[5], 71), 0),
        "w_qkv": draw_w_qkv(jax.random.fold_in(keys[5], 71), 0),
        "w_out": scatter_about(keys[2], (D, D), (D // 8) ** -0.5, 0.5, ((0, 8),)),
        "layout": draw_layout(jax.random.fold_in(keys[5], 71), 0),
        "counts": draw_counts(jax.random.fold_in(keys[5], 71), 0),
    }


def attend(query, own_blocks, picked, used):
    block_count = picked.shape[0]
    feature_width = query.shape[1]
    head_width = feature_width // HEADS
    keyvals = jnp.concatenate([own_blocks[:, None], picked], axis=1)
    keyvals = keyvals.reshape(block_count, (KEY_BLOCKS + 1) * BLOCK, 2 * feature_width)
    key_heads = keyvals[..., :feature_width].reshape(block_count, -1, HEADS, head_width)
    value_heads = keyvals[..., feature_width:].reshape(block_count, -1, HEADS, head_width)
    query_heads = query.reshape(block_count, BLOCK, HEADS, head_width)
    scores = jnp.einsum('bqhd,bkhd->bhqk', query_heads.astype(jnp.float32), key_heads.astype(jnp.float32))
    scores = scores * (head_width ** -0.5)
    slot_number = jnp.arange((KEY_BLOCKS + 1) * BLOCK, dtype=jnp.int32) // BLOCK
    usable = slot_number[None, :] <= used[:, None]
    scores = jnp.where(usable[:, None, None, :], scores, -jnp.inf)
    largest = jnp.max(scores, axis=-1, keepdims=True)
    expons = jnp.exp(scores - largest)
    denominator = jnp.sum(expons, axis=-1, keepdims=True)
    rounded = lax.optimization_barrier(expons.astype(jnp.bfloat16)).astype(jnp.float32)
    summed = jnp.einsum('bhqk,bkhd->bqhd', rounded, value_heads.astype(jnp.float32))
    summed = summed / jnp.transpose(denominator, (0, 2, 1, 3))
    return summed.reshape(block_count * BLOCK, feature_width).astype(jnp.bfloat16)


def reference(normed, w_qkv, w_out, layout, counts):
    stations = N_SEQ * N_FSDP
    blocks_here = ROWS_DEV // BLOCK
    shards = normed.reshape(stations, ROWS_DEV, D)
    key_weights = w_qkv[:, D:]
    query_weights = w_qkv[:, :D]

    def project_keys(shard):
        return jnp.dot(shard, key_weights, preferred_element_type=jnp.float32).astype(jnp.bfloat16)

    keyvals = lax.map(project_keys, shards)

    def one_station(station):
        span_pos = station // N_FSDP
        stream_pos = station % N_FSDP
        lower = ((span_pos - 1) % N_SEQ) * N_FSDP + stream_pos
        upper = ((span_pos + 1) % N_SEQ) * N_FSDP + stream_pos
        query = jnp.dot(shards[station], query_weights, preferred_element_type=jnp.float32).astype(jnp.bfloat16)
        pool = jnp.concatenate([keyvals[lower], keyvals[station], keyvals[upper]], axis=0)
        pool = pool.reshape(3 * blocks_here, BLOCK, 2 * D)
        first_block = (station * blocks_here).astype(jnp.int32)
        layout_here = lax.dynamic_slice_in_dim(layout, first_block, blocks_here, 0)
        counts_here = lax.dynamic_slice_in_dim(counts, first_block, blocks_here, 0)
        own_blocks = pool[blocks_here:2 * blocks_here]
        picked = pool[layout_here]
        attended = attend(query, own_blocks, picked, counts_here)
        return jnp.dot(attended, w_out, preferred_element_type=jnp.float32).astype(jnp.bfloat16)

    mixed = lax.map(one_station, jnp.arange(stations, dtype=jnp.int32))
    return mixed.reshape(TOKENS, D)
```

```python
import functools

import jax
import jax.numpy as jnp
from jax import lax
from jax.experimental import pallas as pl
from jax.experimental.pallas import tpu as pltpu
from jax.sharding import PartitionSpec as P

HEADS = 8
BLOCK = 128
HEAD = 128
MESH = pl.DeviceIdType.MESH
LOG2E = 1.4426950408889634
NEG = float("-inf")
F32 = jnp.float32
BF16 = jnp.bfloat16


def from_behind(value, axis, steps):
    count = lax.axis_size(axis)
    pairs = [(source, (source + steps) % count) for source in range(count)]
    return lax.ppermute(value, axis, pairs)


def gather_kernel(wq, wo, gq, go, send, recv, send2, recv2, own):
    s = lax.axis_index("seq")
    f = lax.axis_index("fsdp")
    core = lax.rem(s, 2)
    mate = (s + 1 - 2 * core, f)
    y = lax.rem(f, 2)
    z = f // 2
    up, down, far = lax.rem(z + 1, 4), lax.rem(z + 3, 4), lax.rem(z + 2, 4)
    dev_y, dev_up, dev_down = (s, 2 * z + 1 - y), (s, 2 * up + y), (s, 2 * down + y)
    barrier = pltpu.get_barrier_semaphore()
    for peer in (dev_y, dev_up, dev_down, mate):
        pl.semaphore_signal(barrier, inc=1, device_id=peer, device_id_type=MESH)
    pl.semaphore_wait(barrier, 4)
    rows = gq.shape[0] // 8
    half = rows // 2

    started = []
    for a, (w, g) in enumerate(((wq, gq), (wo, go))):
        mine = pltpu.make_async_copy(w, g.at[pl.ds(pl.multiple_of(f * rows, rows), rows)], own.at[a])
        mine.start()
        started.append(mine)

    def part(owner, offset, count):
        return pl.ds(pl.multiple_of(owner * rows + core * half + offset, 32), count)

    for a, (w, g) in enumerate(((wq, gq), (wo, go))):
        def send_to(k, owner, offset, count, peer, local):
            place = part(owner, offset, count)
            source = w.at[pl.ds(pl.multiple_of(core * half, 32), half)] if local else g.at[place]
            copy = pltpu.make_async_remote_copy(
                source, g.at[place], send.at[a, k], recv.at[a, k], device_id=peer, device_id_type=MESH)
            copy.start()
            return copy

        def hand(k, owner):
            place = part(owner, 0, half)
            copy = pltpu.make_async_remote_copy(
                g.at[place], g.at[place], send2.at[a, k], recv2.at[a, k], device_id=mate, device_id_type=MESH)
            copy.start()
            return copy

        own_y = 2 * z + 1 - y
        c_y = send_to(0, f, 0, half, dev_y, True)
        c_u0 = send_to(1, f, 0, half, dev_up, True)
        c_d0 = send_to(2, f, 0, half, dev_down, True)
        c_y.wait_recv()
        c_u1 = send_to(3, own_y, 0, half, dev_up, False)
        c_d1 = send_to(4, own_y, 0, half, dev_down, False)
        hands = [hand(0, own_y)]
        c_u0.wait_recv()
        c_u2 = send_to(5, 2 * down + y, 0, half // 2, dev_up, False)
        hands.append(hand(1, 2 * down + y))
        c_d0.wait_recv()
        c_d2 = send_to(6, 2 * up + y, half // 2, half // 2, dev_down, False)
        hands.append(hand(2, 2 * up + y))
        c_u1.wait_recv()
        c_u3 = send_to(7, 2 * down + 1 - y, 0, half // 2, dev_up, False)
        hands.append(hand(3, 2 * down + 1 - y))
        c_d1.wait_recv()
        c_d3 = send_to(8, 2 * up + 1 - y, half // 2, half // 2, dev_down, False)
        hands.append(hand(4, 2 * up + 1 - y))
        c_u2.wait_recv()
        c_d2.wait_recv()
        hands.append(hand(5, 2 * far + y))
        c_u3.wait_recv()
        c_d3.wait_recv()
        hands.append(hand(6, 2 * far + 1 - y))
        for copy in (c_y, c_u0, c_d0, c_u1, c_d1, c_u2, c_d2, c_u3, c_d3):
            copy.wait_send()
        for copy in hands:
            copy.wait()
    for copy in started:
        copy.wait()


def gather_weights(w_qkv, w_out):
    hbm = pl.BlockSpec(memory_space=pl.ANY)
    dma = pltpu.SemaphoreType.DMA
    return pl.pallas_call(
        gather_kernel,
        out_shape=[
            jax.ShapeDtypeStruct((8 * w_qkv.shape[0], w_qkv.shape[1]), BF16),
            jax.ShapeDtypeStruct((8 * w_out.shape[0], w_out.shape[1]), BF16),
        ],
        in_specs=[hbm, hbm],
        out_specs=[hbm, hbm],
        scratch_shapes=[dma((2, 9)), dma((2, 9)), dma((2, 7)), dma((2, 7)), dma((2,))],
        compiler_params=pltpu.CompilerParams(collective_id=0, has_side_effects=True),
        name="gather_weights",
    )(w_qkv, w_out)


def nt_dot(a, b):
    return lax.dot_general(a, b, (((1,), (1,)), ((), ())), preferred_element_type=F32)


def attention_kernel(layout, counts, q_ref, k_ref, v_ref, wo_ref, o_ref, s_sc, m_sc, l_sc, a_sc, att):
    scale = HEAD ** -0.5 * LOG2E
    lane = lax.broadcasted_iota(jnp.int32, (1, 2 * BLOCK), 1)
    slots = layout.shape[1]

    def block(b, _):
        used = counts[b] + 1
        pairs = (used + 1) // 2
        rows = pl.ds(pl.multiple_of(b * BLOCK, BLOCK), BLOCK)
        for h in range(HEADS):
            m_sc[h] = jnp.full((BLOCK, BLOCK), NEG, F32)
            l_sc[h] = jnp.zeros((BLOCK, BLOCK), F32)
            a_sc[h] = jnp.zeros((BLOCK, HEAD), F32)

        def entries(i):
            first = jnp.where(i == 0, 8 + b, layout[b, jnp.maximum(2 * i - 1, 0)])
            return first, layout[b, jnp.minimum(2 * i, slots - 1)]

        def score(i, _):
            e0, e1 = entries(i)
            bias = jnp.where((lane >= BLOCK) & (2 * i + 1 >= used), NEG, 0.0)
            for h in range(HEADS):
                cols = slice(h * HEAD, (h + 1) * HEAD)
                keys = jnp.concatenate([k_ref[e0, :, cols], k_ref[e1, :, cols]], axis=0)
                s = nt_dot(q_ref[rows, cols], keys) + bias
                s_sc[i, h] = s
                m_sc[h] = jnp.maximum(m_sc[h], jnp.maximum(s[:, :BLOCK], s[:, BLOCK:]))
            return 0

        lax.fori_loop(0, pairs, score, 0)
        for h in range(HEADS):
            m_sc[h] = jnp.broadcast_to(jnp.max(m_sc[h], axis=1, keepdims=True) * scale, (BLOCK, BLOCK))

        def weigh(i, _):
            e0, e1 = entries(i)
            for h in range(HEADS):
                cols = slice(h * HEAD, (h + 1) * HEAD)
                values = jnp.concatenate([v_ref[e0, :, cols], v_ref[e1, :, cols]], axis=0)
                s = s_sc[i, h]
                m = m_sc[h]
                p0 = jnp.exp2(s[:, :BLOCK] * scale - m)
                p1 = jnp.exp2(s[:, BLOCK:] * scale - m)
                l_sc[h] += p0 + p1
                p = jnp.concatenate([p0.astype(BF16), p1.astype(BF16)], axis=1)
                a_sc[h] += jnp.dot(p, values, preferred_element_type=F32)
            return 0

        lax.fori_loop(0, pairs, weigh, 0)
        for h in range(HEADS):
            total = jnp.sum(l_sc[h], axis=1, keepdims=True)
            att[rows, h * HEAD:(h + 1) * HEAD] = (a_sc[h] / total).astype(BF16)
        return 0

    lax.fori_loop(0, q_ref.shape[0] // BLOCK, block, 0)
    for c in range(0, o_ref.shape[1], 256):
        o_ref[:, c:c + 256] = jnp.dot(att[...], wo_ref[:, c:c + 256], preferred_element_type=F32).astype(BF16)


def attention(q, k, v, w_out, layout, counts):
    vmem = pl.BlockSpec(memory_space=pltpu.VMEM)
    smem = pl.BlockSpec(memory_space=pltpu.SMEM)
    pairs = layout.shape[1] // 2 + 1
    return pl.pallas_call(
        attention_kernel,
        out_shape=jax.ShapeDtypeStruct(q.shape, BF16),
        in_specs=[smem, smem, vmem, vmem, vmem, vmem],
        out_specs=vmem,
        scratch_shapes=[
            pltpu.VMEM((pairs, HEADS, BLOCK, 2 * BLOCK), F32),
            pltpu.VMEM((HEADS, BLOCK, BLOCK), F32),
            pltpu.VMEM((HEADS, BLOCK, BLOCK), F32),
            pltpu.VMEM((HEADS, BLOCK, HEAD), F32),
            pltpu.VMEM(q.shape, BF16),
        ],
        compiler_params=pltpu.CompilerParams(vmem_limit_bytes=56 << 20),
        name="attention",
    )(layout, counts, q, k, v, w_out)


def shards(normed, w_qkv, w_out, layout, counts):
    width = normed.shape[1]
    lower = from_behind(normed, "seq", 1)
    upper = from_behind(normed, "seq", -1)
    full_qkv, full_out = gather_weights(w_qkv, w_out)
    pool = jnp.concatenate([lower, normed, upper], axis=0)
    queries = jnp.dot(normed, full_qkv[:, :width], preferred_element_type=F32).astype(BF16)
    keys = jnp.dot(pool, full_qkv[:, width:2 * width], preferred_element_type=F32).astype(BF16)
    values = jnp.dot(pool, full_qkv[:, 2 * width:], preferred_element_type=F32).astype(BF16)
    shape = (-1, BLOCK, width)
    return attention(queries, keys.reshape(shape), values.reshape(shape), full_out, layout, counts)


def solution(mesh):
    return jax.shard_map(
        shards,
        mesh=mesh,
        in_specs=(
            P(("seq", "fsdp"), None),
            P("fsdp", None),
            P("fsdp", None),
            P(("seq", "fsdp"), None),
            P(("seq", "fsdp")),
        ),
        out_specs=P(("seq", "fsdp"), None),
        check_vma=False,
    )
```

```python
import functools

import jax
import jax.numpy as jnp
from jax import lax
from jax.experimental import pallas as pl
from jax.experimental.pallas import tpu as pltpu
from jax.sharding import PartitionSpec as P

HEADS = 8
BLOCK = 128
HEAD = 128
MESH = pl.DeviceIdType.MESH
LOG2E = 1.4426950408889634
NEG = float("-inf")
F32 = jnp.float32
BF16 = jnp.bfloat16


def project_kernel(x, wq_shard, wo_shard, q_out, k_out, v_out, wo_out, wq, inner, outer, stage_q, stage_kv, send, recv,
                   send2, recv2, own, x_send, x_recv, store):
    s = lax.axis_index("seq")
    f = lax.axis_index("fsdp")
    count = lax.axis_size("seq")
    core = lax.rem(s, 2)
    side = 2 * core - 1
    mate = (s - side, f)
    beyond = (lax.rem(s + side + count, count), f)
    y = lax.rem(f, 2)
    z = f // 2
    fy = 2 * z + 1 - y
    s_flip = s + 2 - 4 * lax.rem(s // 2, 2)
    up, down, far = lax.rem(z + 1, 4), lax.rem(z + 3, 4), lax.rem(z + 2, 4)
    dev_y, dev_y2, dev_up, dev_down = (s, fy), (s_flip, fy), (s, 2 * up + y), (s, 2 * down + y)
    barrier = pltpu.get_barrier_semaphore()
    for peer in (dev_y, dev_y2, dev_up, dev_down, mate, beyond):
        pl.semaphore_signal(barrier, inc=1, device_id=peer, device_id_type=MESH)
    pl.semaphore_wait(barrier, 6)
    rows = wq_shard.shape[0]
    half = rows // 2
    quarter = rows // 4
    arrays = ((wq_shard, wq), (wo_shard, wo_out))
    pending = []

    def start(copy):
        copy.start()
        return copy

    def part(owner, offset, size):
        return pl.ds(pl.multiple_of(owner * rows + core * half + offset, quarter), size)

    def send_to(a, k, owner, offset, size, peer, local):
        shard, full = arrays[a]
        place = part(owner, offset, size)
        source = shard.at[pl.ds(pl.multiple_of(core * half + offset, quarter), size)] if local else full.at[place]
        copy = start(pltpu.make_async_remote_copy(
            source, full.at[place], send.at[a, k], recv.at[a, k], device_id=peer, device_id_type=MESH))
        pending.append(copy)
        return copy

    def hand(a, k, owner):
        full = arrays[a][1]
        place = part(owner, 0, half)
        return start(pltpu.make_async_remote_copy(
            full.at[place], full.at[place], send2.at[a, k], recv2.at[a, k], device_id=mate, device_id_type=MESH))

    def send_y(a):
        return (send_to(a, 0, f, 0, quarter, dev_y, True), send_to(a, 9, f, quarter, quarter, dev_y2, True))

    def send_own(a):
        return (send_to(a, 1, f, 0, half, dev_up, True), send_to(a, 2, f, 0, half, dev_down, True))

    def send_other(a):
        return (send_to(a, 3, fy, 0, half, dev_up, False), send_to(a, 4, fy, 0, half, dev_down, False))

    def onward(a, first, odd):
        lane = 1 - y if odd else y
        k = 7 if odd else 5
        h = 3 if odd else 1
        first[0].wait_recv()
        c_up = send_to(a, k, 2 * down + lane, 0, quarter, dev_up, False)
        h_up = hand(a, h, 2 * down + lane)
        first[1].wait_recv()
        c_down = send_to(a, k + 1, 2 * up + lane, quarter, quarter, dev_down, False)
        return (c_up, c_down), [h_up, hand(a, h + 1, 2 * up + lane)]

    def last(a, second, odd):
        second[0].wait_recv()
        second[1].wait_recv()
        return [hand(a, 6 if odd else 5, 2 * far + (1 - y if odd else y))]

    y_q = send_y(0)
    own_q = send_own(0)
    place = pl.ds(pl.multiple_of(f * rows, rows), rows)
    own_copy_q, own_copy_o = [
        start(pltpu.make_async_copy(shard, full.at[place], own.at[a])) for a, (shard, full) in enumerate(arrays)]
    y_o = send_y(1)
    inner_copy = start(pltpu.make_async_remote_copy(
        x, inner, x_send.at[8], x_recv.at[8], device_id=mate, device_id_type=MESH))
    for copy in y_q:
        copy.wait_recv()
    other_q = send_other(0)
    hands_q = [hand(0, 0, fy)]
    for copy in y_o:
        copy.wait_recv()
    step = x.shape[0] // 8
    outer_copies = []
    for i in range(8):
        place = pl.ds(i * step, step)
        outer_copies.append(start(pltpu.make_async_remote_copy(
            x.at[place], outer.at[place], x_send.at[i], x_recv.at[i], device_id=beyond, device_id_type=MESH)))
    onward_q, more = onward(0, own_q, False)
    hands_q += more
    onward_q2, more = onward(0, other_q, True)
    hands_q += more
    own_o = send_own(1)
    other_o = send_other(1)
    hands_o = [hand(1, 0, fy)]
    hands_q += last(0, onward_q, False)
    hands_q += last(0, onward_q2, True)
    own_copy_q.wait()
    for copy in hands_q:
        copy.wait_recv()

    width = x.shape[1]
    tile = 256
    total = x.shape[0]

    def project(source, target, offset, columns):
        def one(n, _):
            cols = pl.ds(pl.multiple_of(n * tile, tile), tile)
            w_cols = pl.ds(pl.multiple_of(offset + n * tile, tile), tile)
            target[:, cols] = jnp.dot(source[...], wq[:, w_cols], preferred_element_type=F32).astype(BF16)
            return 0

        lax.fori_loop(0, columns // tile, one, 0)

    stores = []

    def keep(source, target, k):
        copy = pltpu.make_async_copy(source, target, store.at[k])
        copy.start()
        stores.append(copy)

    def keep_kv(source, base, size, k):
        place = pl.ds(pl.multiple_of(base, size), size)
        keep(source.at[:, pl.ds(0, width)], k_out.at[place], k)
        keep(source.at[:, pl.ds(width, width)], v_out.at[place], k + 1)

    project(x, stage_q, 0, width)
    keep(stage_q, q_out, 0)
    onward_o, more = onward(1, own_o, False)
    hands_o += more
    project(x, stage_kv.at[pl.ds(0, total)], width, 2 * width)
    keep_kv(stage_kv.at[pl.ds(0, total)], total, total, 1)
    onward_o2, more = onward(1, other_o, True)
    hands_o += more
    inner_copy.wait_recv()
    project(inner, stage_kv.at[pl.ds(total, total)], width, 2 * width)
    keep_kv(stage_kv.at[pl.ds(total, total)], (1 - core) * 2 * total, total, 3)
    hands_o += last(1, onward_o, False)
    hands_o += last(1, onward_o2, True)
    for i in range(4):
        outer_copies[2 * i].wait_recv()
        outer_copies[2 * i + 1].wait_recv()
        piece = pl.ds(2 * i * step, 2 * step)
        staged = stage_kv.at[pl.ds(2 * total + 2 * i * step, 2 * step)]
        project(outer.at[piece], staged, width, 2 * width)
        keep_kv(staged, core * 2 * total + 2 * i * step, 2 * step, 5 + 2 * i)
    own_copy_o.wait()
    for copy in hands_o:
        copy.wait_recv()
    for copy in pending + hands_q + hands_o + outer_copies + [inner_copy]:
        copy.wait_send()
    for copy in stores:
        copy.wait()


def project_all(x, w_qkv, w_out):
    hbm = pl.BlockSpec(memory_space=pl.ANY)
    vmem = pl.BlockSpec(memory_space=pltpu.VMEM)
    dma = pltpu.SemaphoreType.DMA
    rows, width = x.shape
    return pl.pallas_call(
        project_kernel,
        out_shape=[
            jax.ShapeDtypeStruct((rows, width), BF16),
            jax.ShapeDtypeStruct((3 * rows, width), BF16),
            jax.ShapeDtypeStruct((3 * rows, width), BF16),
            jax.ShapeDtypeStruct((8 * w_out.shape[0], width), BF16),
        ],
        in_specs=[vmem, hbm, hbm],
        out_specs=[hbm, hbm, hbm, hbm],
        scratch_shapes=[
            pltpu.VMEM((8 * w_qkv.shape[0], w_qkv.shape[1]), BF16),
            pltpu.VMEM((rows, width), BF16),
            pltpu.VMEM((rows, width), BF16),
            pltpu.VMEM((rows, width), BF16),
            pltpu.VMEM((3 * rows, 2 * width), BF16),
            dma((2, 10)), dma((2, 10)), dma((2, 7)), dma((2, 7)), dma((2,)), dma((9,)), dma((9,)), dma((13,)),
        ],
        compiler_params=pltpu.CompilerParams(
            collective_id=0, has_side_effects=True, vmem_limit_bytes=48 << 20),
        name="gather_and_project",
    )(x, w_qkv, w_out)


def nt_dot(a, b):
    return lax.dot_general(a, b, (((1,), (1,)), ((), ())), preferred_element_type=F32)


def attention_kernel(layout, counts, q_ref, k_ref, v_ref, wo_ref, o_ref, s_sc, m_sc, l_sc, a_sc, att):
    scale = HEAD ** -0.5 * LOG2E
    lane = lax.broadcasted_iota(jnp.int32, (1, 2 * BLOCK), 1)
    slots = layout.shape[1]

    def block(b, _):
        used = counts[b] + 1
        pairs = (used + 1) // 2
        rows = pl.ds(pl.multiple_of(b * BLOCK, BLOCK), BLOCK)
        for h in range(HEADS):
            m_sc[h] = jnp.full((BLOCK, BLOCK), NEG, F32)
            l_sc[h] = jnp.zeros((BLOCK, BLOCK), F32)
            a_sc[h] = jnp.zeros((BLOCK, HEAD), F32)

        def entries(i):
            first = jnp.where(i == 0, 8 + b, layout[b, jnp.maximum(2 * i - 1, 0)])
            return first, layout[b, jnp.minimum(2 * i, slots - 1)]

        def score(i, _):
            e0, e1 = entries(i)
            bias = jnp.where((lane >= BLOCK) & (2 * i + 1 >= used), NEG, 0.0)
            for h in range(HEADS):
                cols = slice(h * HEAD, (h + 1) * HEAD)
                keys = jnp.concatenate([k_ref[e0, :, cols], k_ref[e1, :, cols]], axis=0)
                s = nt_dot(q_ref[rows, cols], keys) + bias
                s_sc[i, h] = s
                m_sc[h] = jnp.maximum(m_sc[h], jnp.maximum(s[:, :BLOCK], s[:, BLOCK:]))
            return 0

        lax.fori_loop(0, pairs, score, 0)
        for h in range(HEADS):
            m_sc[h] = jnp.broadcast_to(jnp.max(m_sc[h], axis=1, keepdims=True) * scale, (BLOCK, BLOCK))

        def weigh(i, _):
            e0, e1 = entries(i)
            for h in range(HEADS):
                cols = slice(h * HEAD, (h + 1) * HEAD)
                values = jnp.concatenate([v_ref[e0, :, cols], v_ref[e1, :, cols]], axis=0)
                s = s_sc[i, h]
                m = m_sc[h]
                p0 = jnp.exp2(s[:, :BLOCK] * scale - m)
                p1 = jnp.exp2(s[:, BLOCK:] * scale - m)
                l_sc[h] += p0 + p1
                p = jnp.concatenate([p0.astype(BF16), p1.astype(BF16)], axis=1)
                a_sc[h] += jnp.dot(p, values, preferred_element_type=F32)
            return 0

        lax.fori_loop(0, pairs, weigh, 0)
        for h in range(HEADS):
            total = jnp.sum(l_sc[h], axis=1, keepdims=True)
            att[rows, h * HEAD:(h + 1) * HEAD] = (a_sc[h] / total).astype(BF16)
        return 0

    lax.fori_loop(0, q_ref.shape[0] // BLOCK, block, 0)
    for c in range(0, o_ref.shape[1], 256):
        o_ref[:, c:c + 256] = jnp.dot(att[...], wo_ref[:, c:c + 256], preferred_element_type=F32).astype(BF16)


def attention(q, k, v, w_out, layout, counts):
    vmem = pl.BlockSpec(memory_space=pltpu.VMEM)
    smem = pl.BlockSpec(memory_space=pltpu.SMEM)
    pairs = layout.shape[1] // 2 + 1
    return pl.pallas_call(
        attention_kernel,
        out_shape=jax.ShapeDtypeStruct(q.shape, BF16),
        in_specs=[smem, smem, vmem, vmem, vmem, vmem],
        out_specs=vmem,
        scratch_shapes=[
            pltpu.VMEM((pairs, HEADS, BLOCK, 2 * BLOCK), F32),
            pltpu.VMEM((HEADS, BLOCK, BLOCK), F32),
            pltpu.VMEM((HEADS, BLOCK, BLOCK), F32),
            pltpu.VMEM((HEADS, BLOCK, HEAD), F32),
            pltpu.VMEM(q.shape, BF16),
        ],
        compiler_params=pltpu.CompilerParams(vmem_limit_bytes=56 << 20),
        name="attention",
    )(layout, counts, q, k, v, w_out)


def shards(normed, w_qkv, w_out, layout, counts):
    queries, keys, values, full_out = project_all(normed, w_qkv, w_out)
    shape = (-1, BLOCK, normed.shape[1])
    return attention(queries, keys.reshape(shape), values.reshape(shape), full_out, layout, counts)


def solution(mesh):
    return jax.shard_map(
        shards,
        mesh=mesh,
        in_specs=(
            P(("seq", "fsdp"), None),
            P("fsdp", None),
            P("fsdp", None),
            P(("seq", "fsdp"), None),
            P(("seq", "fsdp")),
        ),
        out_specs=P(("seq", "fsdp"), None),
        check_vma=False,
    )
```

```python
import functools

import jax
import jax.numpy as jnp
from jax import lax
from jax.experimental import pallas as pl
from jax.experimental.pallas import tpu as pltpu
from jax.sharding import PartitionSpec as P

HEADS = 8
BLOCK = 128
HEAD = 128
MESH = pl.DeviceIdType.MESH
LOG2E = 1.4426950408889634
NEG = float("-inf")
F32 = jnp.float32
BF16 = jnp.bfloat16


def over_sublanes(value, op):
    result = value[:8]
    for i in range(8, value.shape[0], 8):
        result = op(result, value[i:i + 8])
    return result


def attend_block(layout, counts, b, q_sc, k_sc, vt_sc, score_refs, att):
    scale = HEAD ** -0.5 * LOG2E
    slots = layout.shape[1] + 1
    blocks = q_sc.shape[0]
    pair = 2 * HEAD
    pairs = HEADS // 2
    entry = [blocks + b] + [layout[b, j] for j in range(slots - 1)]
    used = counts[b]
    rows = pl.ds(pl.multiple_of(b * BLOCK, BLOCK), BLOCK)
    zero = jnp.zeros((HEAD, BLOCK), BF16)
    largest = [None] * pairs
    for g in range(-1, pairs):
        ahead = g + 1
        scoring, weighing = ahead < pairs, g >= 0
        if scoring:
            cols = slice(ahead * pair, (ahead + 1) * pair)
            q0 = q_sc[b, :, ahead * pair:ahead * pair + HEAD]
            q1 = q_sc[b, :, ahead * pair + HEAD:(ahead + 1) * pair]
            q_pair = jnp.concatenate(
                [jnp.concatenate([q0.T, zero], 1), jnp.concatenate([zero, q1.T], 1)], 0)
            top = None
        if weighing:
            total = None
            summed = [None, None]
            held = []

        def apply_values():
            for h in range(2):
                head = slice(g * pair + h * HEAD, g * pair + (h + 1) * HEAD)
                left = [vt_sc[entry[i], head, :] for i, _ in held]
                right = [p[:, h * BLOCK:(h + 1) * BLOCK] for _, p in held]
                if len(held) > 1:
                    left, right = [jnp.concatenate(left, 1)], [jnp.concatenate(right, 0)]
                term = jnp.dot(left[0], right[0], preferred_element_type=F32)
                summed[h] = term if summed[h] is None else summed[h] + term
            held.clear()

        for i in range(slots):
            if scoring:
                scores = jnp.dot(k_sc[entry[i], :, cols], q_pair, preferred_element_type=F32)
            if weighing:
                if len(held) == 2:
                    apply_values()
                p = jnp.exp2(score_refs[g % 2][i] * scale - largest[g])
                part = over_sublanes(p, jnp.add)
                total = part if total is None else total + part
                held.append((i, p.astype(BF16)))
            if scoring:
                if i > 1:
                    scores = scores + jnp.where(i <= used, 0.0, NEG)
                score_refs[ahead % 2][i] = scores
                part = over_sublanes(scores, jnp.maximum)
                top = part if top is None else jnp.maximum(top, part)
        if weighing:
            apply_values()
            inverse = 1.0 / jnp.sum(total, axis=0, keepdims=True)
            for h in range(2):
                head = slice(g * pair + h * HEAD, g * pair + (h + 1) * HEAD)
                att[rows, head] = (summed[h] * inverse[:, h * BLOCK:(h + 1) * BLOCK]).T.astype(BF16)
        if scoring:
            largest[ahead] = jnp.max(top, axis=0, keepdims=True) * scale


def sublayer_kernel(layout, counts, x_hbm, wq_shard, wo_shard, out, x, wq, wo, inner, outer, q_sc, k_sc, vt_sc, s0_sc,
                    s1_sc, att, send, recv, send2, recv2, own, x_send, x_recv):
    s = lax.axis_index("seq")
    f = lax.axis_index("fsdp")
    count = lax.axis_size("seq")
    core = lax.rem(s, 2)
    side = 2 * core - 1
    mate = (s - side, f)
    beyond = (lax.rem(s + side + count, count), f)
    y = lax.rem(f, 2)
    z = f // 2
    fy = 2 * z + 1 - y
    s_flip = s + 2 - 4 * lax.rem(s // 2, 2)
    up, down, far = lax.rem(z + 1, 4), lax.rem(z + 3, 4), lax.rem(z + 2, 4)
    dev_y, dev_y2, dev_up, dev_down = (s, fy), (s_flip, fy), (s, 2 * up + y), (s, 2 * down + y)
    barrier = pltpu.get_barrier_semaphore()
    for peer in (dev_y, dev_y2, dev_up, dev_down, mate, beyond):
        pl.semaphore_signal(barrier, inc=1, device_id=peer, device_id_type=MESH)
    pl.semaphore_wait(barrier, 6)
    rows = wq_shard.shape[0]
    half = rows // 2
    quarter = rows // 4
    arrays = ((wq_shard, wq), (wo_shard, wo))
    pending = []

    def start(copy):
        copy.start()
        return copy

    def part(owner, offset, size):
        return pl.ds(pl.multiple_of(owner * rows + core * half + offset, quarter), size)

    def send_to(a, k, owner, offset, size, peer, local):
        shard, full = arrays[a]
        place = part(owner, offset, size)
        source = shard.at[pl.ds(pl.multiple_of(core * half + offset, quarter), size)] if local else full.at[place]
        copy = start(pltpu.make_async_remote_copy(
            source, full.at[place], send.at[a, k], recv.at[a, k], device_id=peer, device_id_type=MESH))
        pending.append(copy)
        return copy

    def hand(a, k, owner):
        full = arrays[a][1]
        place = part(owner, 0, half)
        return start(pltpu.make_async_remote_copy(
            full.at[place], full.at[place], send2.at[a, k], recv2.at[a, k], device_id=mate, device_id_type=MESH))

    def send_y(a):
        return (send_to(a, 0, f, 0, quarter, dev_y, True), send_to(a, 9, f, quarter, quarter, dev_y2, True))

    def send_own(a):
        return (send_to(a, 1, f, 0, half, dev_up, True), send_to(a, 2, f, 0, half, dev_down, True))

    def send_other(a):
        return (send_to(a, 3, fy, 0, half, dev_up, False), send_to(a, 4, fy, 0, half, dev_down, False))

    def onward(a, first, odd):
        lane = 1 - y if odd else y
        k = 7 if odd else 5
        h = 3 if odd else 1
        first[0].wait_recv()
        c_up = send_to(a, k, 2 * down + lane, 0, quarter, dev_up, False)
        h_up = hand(a, h, 2 * down + lane)
        first[1].wait_recv()
        c_down = send_to(a, k + 1, 2 * up + lane, quarter, quarter, dev_down, False)
        return (c_up, c_down), [h_up, hand(a, h + 1, 2 * up + lane)]

    def last(a, second, odd):
        second[0].wait_recv()
        second[1].wait_recv()
        return [hand(a, 6 if odd else 5, 2 * far + (1 - y if odd else y))]

    x_copy = start(pltpu.make_async_copy(x_hbm, x, own.at[2]))
    y_q = send_y(0)
    own_q = send_own(0)
    place = pl.ds(pl.multiple_of(f * rows, rows), rows)
    own_copy_q, own_copy_o = [
        start(pltpu.make_async_copy(shard, full.at[place], own.at[a])) for a, (shard, full) in enumerate(arrays)]
    y_o = send_y(1)
    inner_copy = start(pltpu.make_async_remote_copy(
        x_hbm, inner, x_send.at[8], x_recv.at[8], device_id=mate, device_id_type=MESH))
    for copy in y_q:
        copy.wait_recv()
    other_q = send_other(0)
    hands_q = [hand(0, 0, fy)]
    step = x.shape[0] // 8
    outer_copies = []
    for i in range(8):
        place = pl.ds(i * step, step)
        outer_copies.append(start(pltpu.make_async_remote_copy(
            x_hbm.at[place], outer.at[place], x_send.at[i], x_recv.at[i], device_id=beyond, device_id_type=MESH)))
    onward_q, more = onward(0, own_q, False)
    hands_q += more
    onward_q2, more = onward(0, other_q, True)
    hands_q += more
    own_o = send_own(1)
    for copy in y_o:
        copy.wait_recv()
    other_o = send_other(1)
    hands_o = [hand(1, 0, fy)]
    hands_q += last(0, onward_q, False)
    hands_q += last(0, onward_q2, True)
    own_copy_q.wait()
    for copy in hands_q:
        copy.wait_recv()

    x_copy.wait()
    width = x.shape[1]
    tile = 256
    total = x.shape[0]
    blocks = total // BLOCK

    def project(source, target, first, offset):
        def one(n, _):
            w_cols = pl.ds(pl.multiple_of(offset + n * tile, tile), tile)
            value = jnp.dot(source[...], wq[:, w_cols], preferred_element_type=F32).astype(BF16)
            cols = pl.ds(pl.multiple_of(n * tile, tile), tile)
            for j in range(value.shape[0] // BLOCK):
                piece = value[j * BLOCK:(j + 1) * BLOCK]
                if offset == 2 * width:
                    target[first + j, cols, :] = piece.T
                else:
                    target[first + j, :, cols] = piece
            return 0

        lax.fori_loop(0, width // tile, one, 0)

    project(x, q_sc, 0, 0)
    onward_o, more = onward(1, own_o, False)
    hands_o += more
    project(x, k_sc, blocks, width)
    project(x, vt_sc, blocks, 2 * width)
    onward_o2, more = onward(1, other_o, True)
    hands_o += more
    inner_copy.wait_recv()
    inner_first = (1 - core) * 2 * blocks
    project(inner, k_sc, inner_first, width)
    project(inner, vt_sc, inner_first, 2 * width)
    hands_o += last(1, onward_o, False)
    hands_o += last(1, onward_o2, True)
    pieces = 4
    size = total // pieces
    for i in range(pieces):
        for copy in outer_copies[i * 8 // pieces:(i + 1) * 8 // pieces]:
            copy.wait_recv()
        piece = outer.at[pl.ds(i * size, size)]
        first = core * 2 * blocks + i * (size // BLOCK)
        project(piece, k_sc, first, width)
        project(piece, vt_sc, first, 2 * width)

    def block(b, _):
        attend_block(layout, counts, b, q_sc, k_sc, vt_sc, (s0_sc, s1_sc), att)
        return 0

    lax.fori_loop(0, blocks, block, 0)
    own_copy_o.wait()
    for copy in hands_o:
        copy.wait_recv()
    for c in range(0, width, tile):
        out[:, c:c + tile] = jnp.dot(att[...], wo[:, c:c + tile], preferred_element_type=F32).astype(BF16)
    for copy in pending + hands_q + hands_o + outer_copies + [inner_copy]:
        copy.wait_send()


def shards(normed, w_qkv, w_out, layout, counts):
    hbm = pl.BlockSpec(memory_space=pl.ANY)
    smem = pl.BlockSpec(memory_space=pltpu.SMEM)
    vmem = pl.BlockSpec(memory_space=pltpu.VMEM)
    dma = pltpu.SemaphoreType.DMA
    rows, width = normed.shape
    blocks = rows // BLOCK
    slots = layout.shape[1] + 1
    return pl.pallas_call(
        sublayer_kernel,
        out_shape=jax.ShapeDtypeStruct((rows, width), BF16),
        in_specs=[smem, smem, hbm, hbm, hbm],
        out_specs=vmem,
        scratch_shapes=[
            pltpu.VMEM((rows, width), BF16),
            pltpu.VMEM((8 * w_qkv.shape[0], w_qkv.shape[1]), BF16),
            pltpu.VMEM((8 * w_out.shape[0], w_out.shape[1]), BF16),
            pltpu.VMEM((rows, width), BF16),
            pltpu.VMEM((rows, width), BF16),
            pltpu.VMEM((blocks, BLOCK, width), BF16),
            pltpu.VMEM((3 * blocks, BLOCK, width), BF16),
            pltpu.VMEM((3 * blocks, width, BLOCK), BF16),
            pltpu.VMEM((slots, BLOCK, 2 * HEAD), F32),
            pltpu.VMEM((slots, BLOCK, 2 * HEAD), F32),
            pltpu.VMEM((rows, width), BF16),
            dma((2, 10)), dma((2, 10)), dma((2, 7)), dma((2, 7)), dma((3,)), dma((9,)), dma((9,)),
        ],
        compiler_params=pltpu.CompilerParams(
            collective_id=0, has_side_effects=True, vmem_limit_bytes=60 << 20),
        name="sublayer",
    )(layout, counts, normed, w_qkv, w_out)


def solution(mesh):
    return jax.shard_map(
        shards,
        mesh=mesh,
        in_specs=(
            P(("seq", "fsdp"), None),
            P("fsdp", None),
            P("fsdp", None),
            P(("seq", "fsdp"), None),
            P(("seq", "fsdp")),
        ),
        out_specs=P(("seq", "fsdp"), None),
        check_vma=False,
    )
```

```python
import functools

import jax
import jax.numpy as jnp
from jax import lax
from jax.experimental import pallas as pl
from jax.experimental.pallas import tpu as pltpu
from jax.sharding import PartitionSpec as P

HEADS = 8
BLOCK = 128
HEAD = 128
MESH = pl.DeviceIdType.MESH
LOG2E = 1.4426950408889634
NEG = float("-inf")
F32 = jnp.float32
BF16 = jnp.bfloat16


def over_sublanes(value, op):
    result = value[:8]
    for i in range(8, value.shape[0], 8):
        result = op(result, value[i:i + 8])
    return result


def score_and_weigh(layout, counts, scored, weighed, q_sc, k_sc, vt_sc, score_refs, top_sc, att):
    slots = layout.shape[1] + 1
    blocks = q_sc.shape[0]
    pair = 2 * HEAD
    zero = jnp.zeros((HEAD, BLOCK), BF16)

    def entries(b):
        return [blocks + b] + [layout[b, j] for j in range(slots - 1)]

    if scored is not None:
        b, g, buffer = scored
        entry = entries(b)
        used = counts[b]
        q0 = q_sc[b, :, g * pair:g * pair + HEAD]
        q1 = q_sc[b, :, g * pair + HEAD:(g + 1) * pair]
        q_pair = jnp.concatenate([jnp.concatenate([q0.T, zero], 1), jnp.concatenate([zero, q1.T], 1)], 0)
        top = None
    if weighed is not None:
        b2, g2, buffer2 = weighed
        entry2 = entries(b2)
        largest = top_sc[buffer2]
        largest = largest[0:1]
        total = None
        summed = [None, None]
        held = []

    def head_rows(h):
        return slice(g2 * pair + h * HEAD, g2 * pair + (h + 1) * HEAD)

    def apply_values():
        for h in range(2):
            left = [vt_sc[entry2[i], head_rows(h), :] for i, _ in held]
            right = [p[:, h * BLOCK:(h + 1) * BLOCK] for _, p in held]
            if len(held) > 1:
                left, right = [jnp.concatenate(left, 1)], [jnp.concatenate(right, 0)]
            term = jnp.dot(left[0], right[0], preferred_element_type=F32)
            summed[h] = term if summed[h] is None else summed[h] + term
        held.clear()

    for i in range(slots):
        if scored is not None:
            scores = jnp.dot(
                k_sc[entry[i], :, g * pair:(g + 1) * pair], q_pair, preferred_element_type=F32)
        if weighed is not None:
            if len(held) == 2:
                apply_values()
            p = jnp.exp2(score_refs[buffer2][i] - largest)
            part = over_sublanes(p, jnp.add)
            total = part if total is None else total + part
            held.append((i, p.astype(BF16)))
        if scored is not None:
            if i > 1:
                scores = scores + jnp.where(i <= used, 0.0, NEG)
            score_refs[buffer][i] = scores
            part = over_sublanes(scores, jnp.maximum)
            top = part if top is None else jnp.maximum(top, part)
    if weighed is not None:
        apply_values()
        inverse = 1.0 / jnp.sum(total, axis=0, keepdims=True)
        rows = pl.ds(pl.multiple_of(b2 * BLOCK, BLOCK), BLOCK)
        for h in range(2):
            att[rows, head_rows(h)] = (summed[h] * inverse[:, h * BLOCK:(h + 1) * BLOCK]).T.astype(BF16)
    if scored is not None:
        top_sc[buffer] = jnp.broadcast_to(jnp.max(top, axis=0, keepdims=True), top.shape)


def sublayer_kernel(layout, counts, x_hbm, wq_shard, wo_shard, out, x, wq, wo, inner, outer, q_sc, k_sc, vt_sc, s0_sc,
                    s1_sc, top_sc, att, send, recv, send2, recv2, own, x_send, x_recv):
    s = lax.axis_index("seq")
    f = lax.axis_index("fsdp")
    count = lax.axis_size("seq")
    core = lax.rem(s, 2)
    side = 2 * core - 1
    mate = (s - side, f)
    beyond = (lax.rem(s + side + count, count), f)
    y = lax.rem(f, 2)
    z = f // 2
    fy = 2 * z + 1 - y
    s_flip = s + 2 - 4 * lax.rem(s // 2, 2)
    up, down, far = lax.rem(z + 1, 4), lax.rem(z + 3, 4), lax.rem(z + 2, 4)
    dev_y = (jnp.where(core == 0, s, s_flip), fy)
    dev_up, dev_down = (s, 2 * up + y), (s, 2 * down + y)
    x_count = 4
    stride = count // x_count
    x_pos = s // stride
    along_x = [(lax.rem(s + k * stride, count), f) for k in range(1, x_count)]
    barrier = pltpu.get_barrier_semaphore()
    for peer in [dev_y, dev_up, dev_down, mate, beyond] + along_x:
        pl.semaphore_signal(barrier, inc=1, device_id=peer, device_id_type=MESH)
    pl.semaphore_wait(barrier, 5 + len(along_x))
    rows = wq_shard.shape[0]
    half = rows // 2
    quarter = rows // 4
    slice_rows = half // x_count
    arrays = ((wq_shard, wq), (wo_shard, wo))
    pending = []

    def start(copy):
        copy.start()
        return copy

    def part(owner, offset, size):
        return pl.ds(pl.multiple_of(owner * rows + core * half + offset, slice_rows), size)

    def send_to(a, k, owner, offset, size, peer, local):
        shard, full = arrays[a]
        place = part(owner, offset, size)
        source = shard.at[pl.ds(pl.multiple_of(core * half + offset, slice_rows), size)] if local else full.at[place]
        copy = start(pltpu.make_async_remote_copy(
            source, full.at[place], send.at[a, k], recv.at[a, k], device_id=peer, device_id_type=MESH))
        pending.append(copy)
        return copy

    def hand(a, k, owner):
        full = arrays[a][1]
        place = part(owner, 0, half)
        return start(pltpu.make_async_remote_copy(
            full.at[place], full.at[place], send2.at[a, k], recv2.at[a, k], device_id=mate, device_id_type=MESH))

    def send_y(a):
        return send_to(a, 0, f, x_pos * slice_rows, slice_rows, dev_y, True)

    def spread(a, first):
        first.wait_recv()
        return [send_to(a, 9 + k, fy, x_pos * slice_rows, slice_rows, peer, False) for k, peer in enumerate(along_x)]

    def send_own(a):
        return (send_to(a, 1, f, 0, half, dev_up, True), send_to(a, 2, f, 0, half, dev_down, True))

    def send_other(a):
        return (send_to(a, 3, fy, 0, half, dev_up, False), send_to(a, 4, fy, 0, half, dev_down, False))

    def onward(a, first, odd):
        lane = 1 - y if odd else y
        k = 7 if odd else 5
        h = 3 if odd else 1
        first[0].wait_recv()
        c_up = send_to(a, k, 2 * down + lane, 0, quarter, dev_up, False)
        h_up = hand(a, h, 2 * down + lane)
        first[1].wait_recv()
        c_down = send_to(a, k + 1, 2 * up + lane, quarter, quarter, dev_down, False)
        return (c_up, c_down), [h_up, hand(a, h + 1, 2 * up + lane)]

    def last(a, second, odd):
        second[0].wait_recv()
        second[1].wait_recv()
        return [hand(a, 6 if odd else 5, 2 * far + (1 - y if odd else y))]

    x_copy = start(pltpu.make_async_copy(x_hbm, x, own.at[2]))
    y_q = send_y(0)
    own_q = send_own(0)
    place = pl.ds(pl.multiple_of(f * rows, rows), rows)
    own_copy_q, own_copy_o = [
        start(pltpu.make_async_copy(shard, full.at[place], own.at[a])) for a, (shard, full) in enumerate(arrays)]
    y_o = send_y(1)
    inner_copy = start(pltpu.make_async_remote_copy(
        x_hbm, inner, x_send.at[8], x_recv.at[8], device_id=mate, device_id_type=MESH))
    spread_q = spread(0, y_q)
    step = x.shape[0] // 8
    outer_copies = []
    for i in range(8):
        place = pl.ds(i * step, step)
        outer_copies.append(start(pltpu.make_async_remote_copy(
            x_hbm.at[place], outer.at[place], x_send.at[i], x_recv.at[i], device_id=beyond, device_id_type=MESH)))
    for copy in spread_q:
        copy.wait_recv()
    other_q = send_other(0)
    hands_q = [hand(0, 0, fy)]
    onward_q, more = onward(0, own_q, False)
    hands_q += more
    onward_q2, more = onward(0, other_q, True)
    hands_q += more
    hands_q += last(0, onward_q, False)
    hands_q += last(0, onward_q2, True)
    spread_o = spread(1, y_o)
    own_o = send_own(1)
    for copy in spread_o:
        copy.wait_recv()
    other_o = send_other(1)
    hands_o = [hand(1, 0, fy)]
    own_copy_q.wait()
    for copy in hands_q:
        copy.wait_recv()

    x_copy.wait()
    width = x.shape[1]
    tile = 256
    total = x.shape[0]
    blocks = total // BLOCK

    def project(source, target, first, offset):
        def one(n, _):
            w_cols = pl.ds(pl.multiple_of(offset + n * tile, tile), tile)
            value = jnp.dot(source[...], wq[:, w_cols], preferred_element_type=F32)
            if offset == 0:
                value = value * (HEAD ** -0.5 * LOG2E)
            value = value.astype(BF16)
            cols = pl.ds(pl.multiple_of(n * tile, tile), tile)
            for j in range(value.shape[0] // BLOCK):
                piece = value[j * BLOCK:(j + 1) * BLOCK]
                if offset == 2 * width:
                    target[first + j, cols, :] = piece.T
                else:
                    target[first + j, :, cols] = piece
            return 0

        lax.fori_loop(0, width // tile, one, 0)

    project(x, q_sc, 0, 0)
    onward_o, more = onward(1, own_o, False)
    hands_o += more
    project(x, k_sc, blocks, width)
    project(x, vt_sc, blocks, 2 * width)
    onward_o2, more = onward(1, other_o, True)
    hands_o += more
    inner_copy.wait_recv()
    inner_first = (1 - core) * 2 * blocks
    project(inner, k_sc, inner_first, width)
    project(inner, vt_sc, inner_first, 2 * width)
    hands_o += last(1, onward_o, False)
    hands_o += last(1, onward_o2, True)
    pieces = 4
    size = total // pieces
    for i in range(pieces):
        for copy in outer_copies[i * 8 // pieces:(i + 1) * 8 // pieces]:
            copy.wait_recv()
        piece = outer.at[pl.ds(i * size, size)]
        first = core * 2 * blocks + i * (size // BLOCK)
        project(piece, k_sc, first, width)
        project(piece, vt_sc, first, 2 * width)

    def step(scored, weighed):
        score_and_weigh(layout, counts, scored, weighed, q_sc, k_sc, vt_sc, (s0_sc, s1_sc), top_sc, att)

    pairs = HEADS // 2

    def block(b, _):
        for g in range(pairs):
            following = (b, g + 1) if g + 1 < pairs else (jnp.minimum(b + 1, blocks - 1), 0)
            step(following + ((g + 1) % 2,), (b, g, g % 2))
        return 0

    step((0, 0, 0), None)
    lax.fori_loop(0, blocks, block, 0)
    own_copy_o.wait()
    for copy in hands_o:
        copy.wait_recv()
    for c in range(0, width, tile):
        out[:, c:c + tile] = jnp.dot(att[...], wo[:, c:c + tile], preferred_element_type=F32).astype(BF16)
    for copy in pending + hands_q + hands_o + outer_copies + [inner_copy]:
        copy.wait_send()


def shards(normed, w_qkv, w_out, layout, counts):
    hbm = pl.BlockSpec(memory_space=pl.ANY)
    smem = pl.BlockSpec(memory_space=pltpu.SMEM)
    vmem = pl.BlockSpec(memory_space=pltpu.VMEM)
    dma = pltpu.SemaphoreType.DMA
    rows, width = normed.shape
    blocks = rows // BLOCK
    slots = layout.shape[1] + 1
    return pl.pallas_call(
        sublayer_kernel,
        out_shape=jax.ShapeDtypeStruct((rows, width), BF16),
        in_specs=[smem, smem, hbm, hbm, hbm],
        out_specs=vmem,
        scratch_shapes=[
            pltpu.VMEM((rows, width), BF16),
            pltpu.VMEM((8 * w_qkv.shape[0], w_qkv.shape[1]), BF16),
            pltpu.VMEM((8 * w_out.shape[0], w_out.shape[1]), BF16),
            pltpu.VMEM((rows, width), BF16),
            pltpu.VMEM((rows, width), BF16),
            pltpu.VMEM((blocks, BLOCK, width), BF16),
            pltpu.VMEM((3 * blocks, BLOCK, width), BF16),
            pltpu.VMEM((3 * blocks, width, BLOCK), BF16),
            pltpu.VMEM((slots, BLOCK, 2 * HEAD), F32),
            pltpu.VMEM((slots, BLOCK, 2 * HEAD), F32),
            pltpu.VMEM((2, 8, 2 * HEAD), F32),
            pltpu.VMEM((rows, width), BF16),
            dma((2, 12)), dma((2, 12)), dma((2, 7)), dma((2, 7)), dma((3,)), dma((9,)), dma((9,)),
        ],
        compiler_params=pltpu.CompilerParams(
            collective_id=0, has_side_effects=True, vmem_limit_bytes=60 << 20),
        name="sublayer",
    )(layout, counts, normed, w_qkv, w_out)


def solution(mesh):
    return jax.shard_map(
        shards,
        mesh=mesh,
        in_specs=(
            P(("seq", "fsdp"), None),
            P("fsdp", None),
            P("fsdp", None),
            P(("seq", "fsdp"), None),
            P(("seq", "fsdp")),
        ),
        out_specs=P(("seq", "fsdp"), None),
        check_vma=False,
    )
```

```python
import functools

import jax
import jax.numpy as jnp
from jax import lax
from jax.experimental import pallas as pl
from jax.experimental.pallas import tpu as pltpu
from jax.sharding import PartitionSpec as P

HEADS = 8
BLOCK = 128
HEAD = 128
MESH = pl.DeviceIdType.MESH
LOG2E = 1.4426950408889634
NEG = float("-inf")
F32 = jnp.float32
BF16 = jnp.bfloat16


def over_sublanes(value, op):
    result = value[:8]
    for i in range(8, value.shape[0], 8):
        result = op(result, value[i:i + 8])
    return result


def score_and_weigh(layout, counts, scored, weighed, q_sc, k_sc, vt_sc, score_refs, top_sc, att):
    scale = HEAD ** -0.5 * LOG2E
    slots = layout.shape[1] + 1
    blocks = q_sc.shape[0]
    pair = 2 * HEAD
    zero = jnp.zeros((HEAD, BLOCK), BF16)

    def entries(b):
        return [blocks + b] + [layout[b, j] for j in range(slots - 1)]

    if scored is not None:
        b, g, buffer = scored
        entry = entries(b)
        used = counts[b]
        q0 = q_sc[b, :, g * pair:g * pair + HEAD]
        q1 = q_sc[b, :, g * pair + HEAD:(g + 1) * pair]
        q_pair = jnp.concatenate([jnp.concatenate([q0.T, zero], 1), jnp.concatenate([zero, q1.T], 1)], 0)
        top = None
    if weighed is not None:
        b2, g2, buffer2 = weighed
        entry2 = entries(b2)
        largest = top_sc[buffer2]
        largest = largest[0:1]
        total = None
        summed = [None, None]
        held = []

    def head_rows(h):
        return slice(g2 * pair + h * HEAD, g2 * pair + (h + 1) * HEAD)

    def apply_values():
        for h in range(2):
            left = [vt_sc[entry2[i], head_rows(h), :] for i, _ in held]
            right = [p[:, h * BLOCK:(h + 1) * BLOCK] for _, p in held]
            if len(held) > 1:
                left, right = [jnp.concatenate(left, 1)], [jnp.concatenate(right, 0)]
            term = jnp.dot(left[0], right[0], preferred_element_type=F32)
            summed[h] = term if summed[h] is None else summed[h] + term
        held.clear()

    for i in range(slots):
        if scored is not None:
            scores = jnp.dot(
                k_sc[entry[i], :, g * pair:(g + 1) * pair], q_pair, preferred_element_type=F32)
        if weighed is not None:
            if len(held) == 2:
                apply_values()
            p = jnp.exp2(score_refs[buffer2][i] * scale - largest)
            part = over_sublanes(p, jnp.add)
            total = part if total is None else total + part
            held.append((i, p.astype(BF16)))
        if scored is not None:
            if i > 1:
                scores = scores + jnp.where(i <= used, 0.0, NEG)
            score_refs[buffer][i] = scores
            part = over_sublanes(scores, jnp.maximum)
            top = part if top is None else jnp.maximum(top, part)
    if weighed is not None:
        apply_values()
        inverse = 1.0 / jnp.sum(total, axis=0, keepdims=True)
        rows = pl.ds(pl.multiple_of(b2 * BLOCK, BLOCK), BLOCK)
        for h in range(2):
            att[rows, head_rows(h)] = (summed[h] * inverse[:, h * BLOCK:(h + 1) * BLOCK]).T.astype(BF16)
    if scored is not None:
        top_sc[buffer] = jnp.broadcast_to(jnp.max(top, axis=0, keepdims=True) * scale, top.shape)


def sublayer_kernel(layout, counts, x_hbm, wq_shard, wo_shard, out, x, wq, wo, inner, outer, q_sc, k_sc, vt_sc, s0_sc,
                    s1_sc, top_sc, att, own_sums, inner_sums, send, recv, send2, recv2, own, x_send, x_recv):
    s = lax.axis_index("seq")
    f = lax.axis_index("fsdp")
    count = lax.axis_size("seq")
    core = lax.rem(s, 2)
    side = 2 * core - 1
    mate = (s - side, f)
    beyond = (lax.rem(s + side + count, count), f)
    y = lax.rem(f, 2)
    z = f // 2
    fy = 2 * z + 1 - y
    s_flip = s + 2 - 4 * lax.rem(s // 2, 2)
    up, down, far = lax.rem(z + 1, 4), lax.rem(z + 3, 4), lax.rem(z + 2, 4)
    dev_y = (jnp.where(core == 0, s, s_flip), fy)
    dev_up, dev_down = (s, 2 * up + y), (s, 2 * down + y)
    x_count = 4
    stride = count // x_count
    x_pos = s // stride
    along_x = [(lax.rem(s + k * stride, count), f) for k in range(1, x_count)]
    barrier = pltpu.get_barrier_semaphore()
    for peer in [dev_y, dev_up, dev_down, mate, beyond] + along_x:
        pl.semaphore_signal(barrier, inc=1, device_id=peer, device_id_type=MESH)
    pl.semaphore_wait(barrier, 5 + len(along_x))
    rows = wq_shard.shape[0]
    half = rows // 2
    quarter = rows // 4
    slice_rows = half // x_count
    arrays = ((wq_shard, wq), (wo_shard, wo))
    pending = []

    def start(copy):
        copy.start()
        return copy

    def part(owner, offset, size):
        return pl.ds(pl.multiple_of(owner * rows + core * half + offset, slice_rows), size)

    def send_to(a, k, owner, offset, size, peer, local):
        shard, full = arrays[a]
        place = part(owner, offset, size)
        source = shard.at[pl.ds(pl.multiple_of(core * half + offset, slice_rows), size)] if local else full.at[place]
        copy = start(pltpu.make_async_remote_copy(
            source, full.at[place], send.at[a, k], recv.at[a, k], device_id=peer, device_id_type=MESH))
        pending.append(copy)
        return copy

    def hand(a, k, owner):
        full = arrays[a][1]
        place = part(owner, 0, half)
        return start(pltpu.make_async_remote_copy(
            full.at[place], full.at[place], send2.at[a, k], recv2.at[a, k], device_id=mate, device_id_type=MESH))

    def send_y(a):
        return send_to(a, 0, f, x_pos * slice_rows, slice_rows, dev_y, True)

    def spread(a, first):
        first.wait_recv()
        return [send_to(a, 9 + k, fy, x_pos * slice_rows, slice_rows, peer, False) for k, peer in enumerate(along_x)]

    def send_own(a):
        return (send_to(a, 1, f, 0, half, dev_up, True), send_to(a, 2, f, 0, half, dev_down, True))

    def send_other(a):
        return (send_to(a, 3, fy, 0, half, dev_up, False), send_to(a, 4, fy, 0, half, dev_down, False))

    def onward(a, first, odd):
        lane = 1 - y if odd else y
        k = 7 if odd else 5
        h = 3 if odd else 1
        first[0].wait_recv()
        c_up = send_to(a, k, 2 * down + lane, 0, quarter, dev_up, False)
        h_up = hand(a, h, 2 * down + lane)
        first[1].wait_recv()
        c_down = send_to(a, k + 1, 2 * up + lane, quarter, quarter, dev_down, False)
        return (c_up, c_down), [h_up, hand(a, h + 1, 2 * up + lane)]

    def last(a, second, odd):
        second[0].wait_recv()
        second[1].wait_recv()
        return [hand(a, 6 if odd else 5, 2 * far + (1 - y if odd else y))]

    x_copy = start(pltpu.make_async_copy(x_hbm, x, own.at[2]))
    y_q = send_y(0)
    own_q = send_own(0)
    place = pl.ds(pl.multiple_of(f * rows, rows), rows)
    own_copy_q, own_copy_o = [
        start(pltpu.make_async_copy(shard, full.at[place], own.at[a])) for a, (shard, full) in enumerate(arrays)]
    y_o = send_y(1)
    inner_copy = start(pltpu.make_async_remote_copy(
        x_hbm, inner, x_send.at[8], x_recv.at[8], device_id=mate, device_id_type=MESH))
    spread_q = spread(0, y_q)
    step = x.shape[0] // 8
    outer_copies = []
    for i in range(8):
        place = pl.ds(i * step, step)
        outer_copies.append(start(pltpu.make_async_remote_copy(
            x_hbm.at[place], outer.at[place], x_send.at[i], x_recv.at[i], device_id=beyond, device_id_type=MESH)))
    for copy in spread_q:
        copy.wait_recv()
    other_q = send_other(0)
    hands_q = [hand(0, 0, fy)]
    spread_o = spread(1, y_o)
    onward_q, more = onward(0, own_q, False)
    hands_q += more
    onward_q2, more = onward(0, other_q, True)
    hands_q += more
    width = x.shape[1]
    tile = 256
    total = x.shape[0]
    blocks = total // BLOCK

    early = [pl.ds(pl.multiple_of(2 * pair * rows, 2 * rows), 2 * rows) for pair in (z, up, down)]
    late = pl.ds(pl.multiple_of(2 * far * rows, 2 * rows), 2 * rows)

    def begin(source, sums, offset, base=0):
        def one(n, _):
            w_cols = pl.ds(pl.multiple_of(offset + n * tile, tile), tile)
            s_cols = pl.ds(pl.multiple_of(offset - base + n * tile, tile), tile)
            terms = [
                jnp.dot(source[:, part_rows], wq[part_rows, w_cols], preferred_element_type=F32) for part_rows in early]
            sums[:, s_cols] = terms[0] + terms[1] + terms[2]
            return 0

        lax.fori_loop(0, width // tile, one, 0)

    def project(source, target, first, offset, sums=None, base=0):
        def one(n, _):
            w_cols = pl.ds(pl.multiple_of(offset + n * tile, tile), tile)
            if sums is None:
                value = jnp.dot(source[...], wq[:, w_cols], preferred_element_type=F32)
            else:
                s_cols = pl.ds(pl.multiple_of(offset - base + n * tile, tile), tile)
                value = sums[:, s_cols] + jnp.dot(source[:, late], wq[late, w_cols], preferred_element_type=F32)
            value = value.astype(BF16)
            cols = pl.ds(pl.multiple_of(n * tile, tile), tile)
            for j in range(value.shape[0] // BLOCK):
                piece = value[j * BLOCK:(j + 1) * BLOCK]
                if offset == 2 * width:
                    target[first + j, cols, :] = piece.T
                else:
                    target[first + j, :, cols] = piece
            return 0

        lax.fori_loop(0, width // tile, one, 0)

    x_copy.wait()
    own_copy_q.wait()
    for copy in hands_q:
        copy.wait_recv()
    for third in range(3):
        begin(x, own_sums, third * width)
    last_hands = last(0, onward_q, False) + last(0, onward_q2, True)
    hands_q += last_hands
    own_o = send_own(1)
    for copy in spread_o:
        copy.wait_recv()
    other_o = send_other(1)
    hands_o = [hand(1, 0, fy)]
    inner_copy.wait_recv()
    for third in (1, 2):
        begin(inner, inner_sums, third * width, width)
    for copy in last_hands:
        copy.wait_recv()
    project(x, q_sc, 0, 0, own_sums)
    project(x, k_sc, blocks, width, own_sums)
    onward_o, more = onward(1, own_o, False)
    hands_o += more
    project(x, vt_sc, blocks, 2 * width, own_sums)
    inner_first = (1 - core) * 2 * blocks
    project(inner, k_sc, inner_first, width, inner_sums, width)
    onward_o2, more = onward(1, other_o, True)
    hands_o += more
    project(inner, vt_sc, inner_first, 2 * width, inner_sums, width)
    hands_o += last(1, onward_o, False)
    hands_o += last(1, onward_o2, True)
    pieces = 4
    size = total // pieces
    for i in range(pieces):
        for copy in outer_copies[i * 8 // pieces:(i + 1) * 8 // pieces]:
            copy.wait_recv()
        piece = outer.at[pl.ds(i * size, size)]
        first = core * 2 * blocks + i * (size // BLOCK)
        project(piece, k_sc, first, width)
        project(piece, vt_sc, first, 2 * width)

    def step(scored, weighed):
        score_and_weigh(layout, counts, scored, weighed, q_sc, k_sc, vt_sc, (s0_sc, s1_sc), top_sc, att)

    pairs = HEADS // 2

    def block(b, _):
        for g in range(pairs):
            following = (b, g + 1) if g + 1 < pairs else (jnp.minimum(b + 1, blocks - 1), 0)
            step(following + ((g + 1) % 2,), (b, g, g % 2))
        return 0

    step((0, 0, 0), None)
    lax.fori_loop(0, blocks, block, 0)
    own_copy_o.wait()
    for copy in hands_o:
        copy.wait_recv()
    for c in range(0, width, tile):
        out[:, c:c + tile] = jnp.dot(att[...], wo[:, c:c + tile], preferred_element_type=F32).astype(BF16)
    for copy in pending + hands_q + hands_o + outer_copies + [inner_copy]:
        copy.wait_send()


def shards(normed, w_qkv, w_out, layout, counts):
    hbm = pl.BlockSpec(memory_space=pl.ANY)
    smem = pl.BlockSpec(memory_space=pltpu.SMEM)
    vmem = pl.BlockSpec(memory_space=pltpu.VMEM)
    dma = pltpu.SemaphoreType.DMA
    rows, width = normed.shape
    blocks = rows // BLOCK
    slots = layout.shape[1] + 1
    return pl.pallas_call(
        sublayer_kernel,
        out_shape=jax.ShapeDtypeStruct((rows, width), BF16),
        in_specs=[smem, smem, hbm, hbm, hbm],
        out_specs=vmem,
        scratch_shapes=[
            pltpu.VMEM((rows, width), BF16),
            pltpu.VMEM((8 * w_qkv.shape[0], w_qkv.shape[1]), BF16),
            pltpu.VMEM((8 * w_out.shape[0], w_out.shape[1]), BF16),
            pltpu.VMEM((rows, width), BF16),
            pltpu.VMEM((rows, width), BF16),
            pltpu.VMEM((blocks, BLOCK, width), BF16),
            pltpu.VMEM((3 * blocks, BLOCK, width), BF16),
            pltpu.VMEM((3 * blocks, width, BLOCK), BF16),
            pltpu.VMEM((slots, BLOCK, 2 * HEAD), F32),
            pltpu.VMEM((slots, BLOCK, 2 * HEAD), F32),
            pltpu.VMEM((2, 8, 2 * HEAD), F32),
            pltpu.VMEM((rows, width), BF16),
            pltpu.VMEM((rows, 3 * width), F32),
            pltpu.VMEM((rows, 2 * width), F32),
            dma((2, 12)), dma((2, 12)), dma((2, 7)), dma((2, 7)), dma((3,)), dma((9,)), dma((9,)),
        ],
        compiler_params=pltpu.CompilerParams(
            collective_id=0, has_side_effects=True, vmem_limit_bytes=60 << 20),
        name="sublayer",
    )(layout, counts, normed, w_qkv, w_out)


def solution(mesh):
    return jax.shard_map(
        shards,
        mesh=mesh,
        in_specs=(
            P(("seq", "fsdp"), None),
            P("fsdp", None),
            P("fsdp", None),
            P(("seq", "fsdp"), None),
            P(("seq", "fsdp")),
        ),
        out_specs=P(("seq", "fsdp"), None),
        check_vma=False,
    )
```

```python
import functools

import jax
import jax.numpy as jnp
from jax import lax
from jax.experimental import pallas as pl
from jax.experimental.pallas import tpu as pltpu
from jax.sharding import PartitionSpec as P

HEADS = 8
BLOCK = 128
HEAD = 128
MESH = pl.DeviceIdType.MESH
LOG2E = 1.4426950408889634
NEG = float("-inf")
F32 = jnp.float32
BF16 = jnp.bfloat16


def over_sublanes(value, op):
    result = value[:8]
    for i in range(8, value.shape[0], 8):
        result = op(result, value[i:i + 8])
    return result


def score_and_weigh(layout, counts, scored, weighed, q_sc, k_sc, vt_sc, score_refs, top_sc, att):
    scale = HEAD ** -0.5 * LOG2E
    slots = layout.shape[1] + 1
    blocks = q_sc.shape[0]
    pair = 2 * HEAD
    zero = jnp.zeros((HEAD, BLOCK), BF16)

    def entries(b):
        return [blocks + b] + [layout[b, j] for j in range(slots - 1)]

    if scored is not None:
        b, g, buffer = scored
        entry = entries(b)
        used = counts[b]
        q0 = q_sc[b, :, g * pair:g * pair + HEAD]
        q1 = q_sc[b, :, g * pair + HEAD:(g + 1) * pair]
        q_pair = jnp.concatenate([jnp.concatenate([q0.T, zero], 1), jnp.concatenate([zero, q1.T], 1)], 0)
        top = None
    if weighed is not None:
        b2, g2, buffer2 = weighed
        entry2 = entries(b2)
        largest = top_sc[buffer2]
        largest = largest[0:1]
        total = None
        summed = [None, None]
        held = []

    def head_rows(h):
        return slice(g2 * pair + h * HEAD, g2 * pair + (h + 1) * HEAD)

    def apply_values():
        for h in range(2):
            left = [vt_sc[entry2[i], head_rows(h), :] for i, _ in held]
            right = [p[:, h * BLOCK:(h + 1) * BLOCK] for _, p in held]
            if len(held) > 1:
                left, right = [jnp.concatenate(left, 1)], [jnp.concatenate(right, 0)]
            term = jnp.dot(left[0], right[0], preferred_element_type=F32)
            summed[h] = term if summed[h] is None else summed[h] + term
        held.clear()

    for i in range(slots):
        if scored is not None:
            scores = jnp.dot(
                k_sc[entry[i], :, g * pair:(g + 1) * pair], q_pair, preferred_element_type=F32)
        if weighed is not None:
            if len(held) == 2:
                apply_values()
            p = jnp.exp2(score_refs[buffer2][i] * scale - largest)
            part = over_sublanes(p, jnp.add)
            total = part if total is None else total + part
            held.append((i, p.astype(BF16)))
        if scored is not None:
            if i > 1:
                scores = scores + jnp.where(i <= used, 0.0, NEG)
            score_refs[buffer][i] = scores
            part = over_sublanes(scores, jnp.maximum)
            top = part if top is None else jnp.maximum(top, part)
    if weighed is not None:
        apply_values()
        inverse = 1.0 / jnp.sum(total, axis=0, keepdims=True)
        rows = pl.ds(pl.multiple_of(b2 * BLOCK, BLOCK), BLOCK)
        for h in range(2):
            att[rows, head_rows(h)] = (summed[h] * inverse[:, h * BLOCK:(h + 1) * BLOCK]).T.astype(BF16)
    if scored is not None:
        top_sc[buffer] = jnp.broadcast_to(jnp.max(top, axis=0, keepdims=True) * scale, top.shape)


def sublayer_kernel(layout, counts, x_hbm, wq_shard, wo_shard, out, x, wq, wo, inner, outer, q_sc, k_sc, vt_sc, s0_sc,
                    s1_sc, top_sc, att, own_sums, inner_sums, send, recv, send2, recv2, own, x_send, x_recv):
    s = lax.axis_index("seq")
    f = lax.axis_index("fsdp")
    count = lax.axis_size("seq")
    core = lax.rem(s, 2)
    side = 2 * core - 1
    mate = (s - side, f)
    beyond = (lax.rem(s + side + count, count), f)
    y = lax.rem(f, 2)
    z = f // 2
    fy = 2 * z + 1 - y
    s_flip = s + 2 - 4 * lax.rem(s // 2, 2)
    up, down, far = lax.rem(z + 1, 4), lax.rem(z + 3, 4), lax.rem(z + 2, 4)
    dev_y = (jnp.where(core == 0, s, s_flip), fy)
    dev_up, dev_down = (s, 2 * up + y), (s, 2 * down + y)
    x_count = 4
    stride = count // x_count
    x_pos = s // stride
    along_x = [(lax.rem(s + k * stride, count), f) for k in range(1, x_count)]
    barrier = pltpu.get_barrier_semaphore()
    for peer in [dev_y, dev_up, dev_down, mate, beyond] + along_x:
        pl.semaphore_signal(barrier, inc=1, device_id=peer, device_id_type=MESH)
    pl.semaphore_wait(barrier, 5 + len(along_x))
    rows = wq_shard.shape[0]
    half = rows // 2
    quarter = rows // 4
    slice_rows = half // x_count
    arrays = ((wq_shard, wq), (wo_shard, wo))
    pending = []

    def start(copy):
        copy.start()
        return copy

    def part(owner, offset, size):
        return pl.ds(pl.multiple_of(owner * rows + core * half + offset, slice_rows), size)

    def send_to(a, k, owner, offset, size, peer, local):
        shard, full = arrays[a]
        place = part(owner, offset, size)
        source = shard.at[pl.ds(pl.multiple_of(core * half + offset, slice_rows), size)] if local else full.at[place]
        copy = start(pltpu.make_async_remote_copy(
            source, full.at[place], send.at[a, k], recv.at[a, k], device_id=peer, device_id_type=MESH))
        pending.append(copy)
        return copy

    def hand(a, k, owner):
        full = arrays[a][1]
        place = part(owner, 0, half)
        return start(pltpu.make_async_remote_copy(
            full.at[place], full.at[place], send2.at[a, k], recv2.at[a, k], device_id=mate, device_id_type=MESH))

    def send_y(a):
        return send_to(a, 0, f, x_pos * slice_rows, slice_rows, dev_y, True)

    def spread(a, first):
        first.wait_recv()
        return [send_to(a, 9 + k, fy, x_pos * slice_rows, slice_rows, peer, False) for k, peer in enumerate(along_x)]

    def send_own(a):
        return (send_to(a, 1, f, 0, half, dev_up, True), send_to(a, 2, f, 0, half, dev_down, True))

    def send_other(a):
        return (send_to(a, 3, fy, 0, half, dev_up, False), send_to(a, 4, fy, 0, half, dev_down, False))

    def onward(a, first, odd):
        lane = 1 - y if odd else y
        k = 7 if odd else 5
        h = 3 if odd else 1
        first[0].wait_recv()
        c_up = send_to(a, k, 2 * down + lane, 0, quarter, dev_up, False)
        h_up = hand(a, h, 2 * down + lane)
        first[1].wait_recv()
        c_down = send_to(a, k + 1, 2 * up + lane, quarter, quarter, dev_down, False)
        return (c_up, c_down), [h_up, hand(a, h + 1, 2 * up + lane)]

    def last(a, second, odd):
        second[0].wait_recv()
        second[1].wait_recv()
        return [hand(a, 6 if odd else 5, 2 * far + (1 - y if odd else y))]

    x_copy = start(pltpu.make_async_copy(x_hbm, x, own.at[2]))
    y_q = send_y(0)
    own_q = send_own(0)
    place = pl.ds(pl.multiple_of(f * rows, rows), rows)
    own_copy_q, own_copy_o = [
        start(pltpu.make_async_copy(shard, full.at[place], own.at[a])) for a, (shard, full) in enumerate(arrays)]
    y_o = send_y(1)
    inner_copy = start(pltpu.make_async_remote_copy(
        x_hbm, inner, x_send.at[8], x_recv.at[8], device_id=mate, device_id_type=MESH))
    spread_q = spread(0, y_q)
    step = x.shape[0] // 8
    outer_copies = []
    for i in range(8):
        place = pl.ds(i * step, step)
        outer_copies.append(start(pltpu.make_async_remote_copy(
            x_hbm.at[place], outer.at[place], x_send.at[i], x_recv.at[i], device_id=beyond, device_id_type=MESH)))
    for copy in spread_q:
        copy.wait_recv()
    other_q = send_other(0)
    hands_q = [hand(0, 0, fy)]
    spread_o = spread(1, y_o)
    onward_q, more = onward(0, own_q, False)
    hands_q += more
    onward_q2, more = onward(0, other_q, True)
    hands_q += more
    width = x.shape[1]
    tile = 256
    total = x.shape[0]
    blocks = total // BLOCK

    early = [pl.ds(pl.multiple_of(2 * pair * rows, 2 * rows), 2 * rows) for pair in (z, up, down)]
    late = pl.ds(pl.multiple_of(2 * far * rows, 2 * rows), 2 * rows)

    def begin(source, sums, offset, base=0):
        def one(n, _):
            w_cols = pl.ds(pl.multiple_of(offset + n * tile, tile), tile)
            s_cols = pl.ds(pl.multiple_of(offset - base + n * tile, tile), tile)
            terms = [
                jnp.dot(source[:, part_rows], wq[part_rows, w_cols], preferred_element_type=F32) for part_rows in early]
            sums[:, s_cols] = terms[0] + terms[1] + terms[2]
            return 0

        lax.fori_loop(0, width // tile, one, 0)

    def project(source, target, first, offset, sums=None, base=0):
        def one(n, _):
            w_cols = pl.ds(pl.multiple_of(offset + n * tile, tile), tile)
            if sums is None:
                value = jnp.dot(source[...], wq[:, w_cols], preferred_element_type=F32)
            else:
                s_cols = pl.ds(pl.multiple_of(offset - base + n * tile, tile), tile)
                value = sums[:, s_cols] + jnp.dot(source[:, late], wq[late, w_cols], preferred_element_type=F32)
            value = value.astype(BF16)
            cols = pl.ds(pl.multiple_of(n * tile, tile), tile)
            for j in range(value.shape[0] // BLOCK):
                piece = value[j * BLOCK:(j + 1) * BLOCK]
                if offset == 2 * width:
                    target[first + j, cols, :] = piece.T
                else:
                    target[first + j, :, cols] = piece
            return 0

        lax.fori_loop(0, width // tile, one, 0)

    x_copy.wait()
    own_copy_q.wait()
    for copy in hands_q:
        copy.wait_recv()
    for third in range(3):
        begin(x, own_sums, third * width)
    last_hands = last(0, onward_q, False) + last(0, onward_q2, True)
    hands_q += last_hands
    own_o = send_own(1)
    for copy in spread_o:
        copy.wait_recv()
    other_o = send_other(1)
    hands_o = [hand(1, 0, fy)]
    inner_copy.wait_recv()
    for third in (1, 2):
        begin(inner, inner_sums, third * width, width)
    for copy in last_hands:
        copy.wait_recv()
    project(x, q_sc, 0, 0, own_sums)
    project(x, k_sc, blocks, width, own_sums)
    onward_o, more = onward(1, own_o, False)
    hands_o += more
    project(x, vt_sc, blocks, 2 * width, own_sums)
    inner_first = (1 - core) * 2 * blocks
    project(inner, k_sc, inner_first, width, inner_sums, width)
    onward_o2, more = onward(1, other_o, True)
    hands_o += more
    project(inner, vt_sc, inner_first, 2 * width, inner_sums, width)
    hands_o += last(1, onward_o, False)
    hands_o += last(1, onward_o2, True)
    pieces = 2
    size = total // pieces
    for i in range(pieces):
        for copy in outer_copies[i * 8 // pieces:(i + 1) * 8 // pieces]:
            copy.wait_recv()
        piece = outer.at[pl.ds(i * size, size)]
        first = core * 2 * blocks + i * (size // BLOCK)
        project(piece, k_sc, first, width)
        project(piece, vt_sc, first, 2 * width)

    def step(scored, weighed):
        score_and_weigh(layout, counts, scored, weighed, q_sc, k_sc, vt_sc, (s0_sc, s1_sc), top_sc, att)

    pairs = HEADS // 2

    def block(b, _):
        for g in range(pairs):
            following = (b, g + 1) if g + 1 < pairs else (jnp.minimum(b + 1, blocks - 1), 0)
            step(following + ((g + 1) % 2,), (b, g, g % 2))
        return 0

    step((0, 0, 0), None)
    lax.fori_loop(0, blocks, block, 0)
    own_copy_o.wait()
    for copy in hands_o:
        copy.wait_recv()
    for c in range(0, width, tile):
        out[:, c:c + tile] = jnp.dot(att[...], wo[:, c:c + tile], preferred_element_type=F32).astype(BF16)
    for copy in pending + hands_q + hands_o + outer_copies + [inner_copy]:
        copy.wait_send()


def shards(normed, w_qkv, w_out, layout, counts):
    hbm = pl.BlockSpec(memory_space=pl.ANY)
    smem = pl.BlockSpec(memory_space=pltpu.SMEM)
    vmem = pl.BlockSpec(memory_space=pltpu.VMEM)
    dma = pltpu.SemaphoreType.DMA
    rows, width = normed.shape
    blocks = rows // BLOCK
    slots = layout.shape[1] + 1
    return pl.pallas_call(
        sublayer_kernel,
        out_shape=jax.ShapeDtypeStruct((rows, width), BF16),
        in_specs=[smem, smem, hbm, hbm, hbm],
        out_specs=vmem,
        scratch_shapes=[
            pltpu.VMEM((rows, width), BF16),
            pltpu.VMEM((8 * w_qkv.shape[0], w_qkv.shape[1]), BF16),
            pltpu.VMEM((8 * w_out.shape[0], w_out.shape[1]), BF16),
            pltpu.VMEM((rows, width), BF16),
            pltpu.VMEM((rows, width), BF16),
            pltpu.VMEM((blocks, BLOCK, width), BF16),
            pltpu.VMEM((3 * blocks, BLOCK, width), BF16),
            pltpu.VMEM((3 * blocks, width, BLOCK), BF16),
            pltpu.VMEM((slots, BLOCK, 2 * HEAD), F32),
            pltpu.VMEM((slots, BLOCK, 2 * HEAD), F32),
            pltpu.VMEM((2, 8, 2 * HEAD), F32),
            pltpu.VMEM((rows, width), BF16),
            pltpu.VMEM((rows, 3 * width), F32),
            pltpu.VMEM((rows, 2 * width), F32),
            dma((2, 12)), dma((2, 12)), dma((2, 7)), dma((2, 7)), dma((3,)), dma((9,)), dma((9,)),
        ],
        compiler_params=pltpu.CompilerParams(
            collective_id=0, has_side_effects=True, vmem_limit_bytes=60 << 20),
        name="sublayer",
    )(layout, counts, normed, w_qkv, w_out)


def solution(mesh):
    return jax.shard_map(
        shards,
        mesh=mesh,
        in_specs=(
            P(("seq", "fsdp"), None),
            P("fsdp", None),
            P("fsdp", None),
            P(("seq", "fsdp"), None),
            P(("seq", "fsdp")),
        ),
        out_specs=P(("seq", "fsdp"), None),
        check_vma=False,
    )
```

```python
import functools

import jax
import jax.numpy as jnp
from jax import lax
from jax.experimental import pallas as pl
from jax.experimental.pallas import tpu as pltpu
from jax.sharding import PartitionSpec as P

HEADS = 8
BLOCK = 128
HEAD = 128
MESH = pl.DeviceIdType.MESH
LOG2E = 1.4426950408889634
NEG = float("-inf")
F32 = jnp.float32
BF16 = jnp.bfloat16


def over_sublanes(value, op):
    result = value[:8]
    for i in range(8, value.shape[0], 8):
        result = op(result, value[i:i + 8])
    return result


def score_and_weigh(layout, counts, scored, weighed, q_sc, k_sc, vt_sc, score_refs, top_sc, att):
    scale = HEAD ** -0.5 * LOG2E
    slots = layout.shape[1] + 1
    blocks = q_sc.shape[0]
    pair = 2 * HEAD
    zero = jnp.zeros((HEAD, BLOCK), BF16)

    def entries(b):
        return [blocks + b] + [layout[b, j] for j in range(slots - 1)]

    if scored is not None:
        b, g, buffer = scored
        entry = entries(b)
        used = counts[b]
        q0 = q_sc[b, :, g * pair:g * pair + HEAD]
        q1 = q_sc[b, :, g * pair + HEAD:(g + 1) * pair]
        q_pair = jnp.concatenate([jnp.concatenate([q0.T, zero], 1), jnp.concatenate([zero, q1.T], 1)], 0)
        top = None
    if weighed is not None:
        b2, g2, buffer2 = weighed
        entry2 = entries(b2)
        largest = top_sc[buffer2]
        largest = largest[0:1]
        total = None
        summed = [None, None]
        held = []

    def head_rows(h):
        return slice(g2 * pair + h * HEAD, g2 * pair + (h + 1) * HEAD)

    def apply_values():
        for h in range(2):
            left = [vt_sc[entry2[i], head_rows(h), :] for i, _ in held]
            right = [p[:, h * BLOCK:(h + 1) * BLOCK] for _, p in held]
            if len(held) > 1:
                left, right = [jnp.concatenate(left, 1)], [jnp.concatenate(right, 0)]
            term = jnp.dot(left[0], right[0], preferred_element_type=F32)
            summed[h] = term if summed[h] is None else summed[h] + term
        held.clear()

    for i in range(slots):
        if scored is not None:
            scores = jnp.dot(
                k_sc[entry[i], :, g * pair:(g + 1) * pair], q_pair, preferred_element_type=F32)
        if weighed is not None:
            if len(held) == 2:
                apply_values()
            p = jnp.exp2(score_refs[buffer2][i] * scale - largest)
            part = over_sublanes(p, jnp.add)
            total = part if total is None else total + part
            held.append((i, p.astype(BF16)))
        if scored is not None:
            if i > 1:
                scores = scores + jnp.where(i <= used, 0.0, NEG)
            score_refs[buffer][i] = scores
            part = over_sublanes(scores, jnp.maximum)
            top = part if top is None else jnp.maximum(top, part)
    if weighed is not None:
        apply_values()
        inverse = 1.0 / jnp.sum(total, axis=0, keepdims=True)
        rows = pl.ds(pl.multiple_of(b2 * BLOCK, BLOCK), BLOCK)
        for h in range(2):
            att[rows, head_rows(h)] = (summed[h] * inverse[:, h * BLOCK:(h + 1) * BLOCK]).T.astype(BF16)
    if scored is not None:
        top_sc[buffer] = jnp.broadcast_to(jnp.max(top, axis=0, keepdims=True) * scale, top.shape)


def sublayer_kernel(layout, counts, x_hbm, wq_shard, wo_shard, out, x, wq, wo, inner, outer, q_sc, k_sc, vt_sc, s0_sc,
                    s1_sc, top_sc, att, own_sums, inner_sums, send, recv, send2, recv2, own, x_send, x_recv):
    s = lax.axis_index("seq")
    f = lax.axis_index("fsdp")
    count = lax.axis_size("seq")
    core = lax.rem(s, 2)
    side = 2 * core - 1
    mate = (s - side, f)
    beyond = (lax.rem(s + side + count, count), f)
    y = lax.rem(f, 2)
    z = f // 2
    fy = 2 * z + 1 - y
    s_flip = s + 2 - 4 * lax.rem(s // 2, 2)
    up, down, far = lax.rem(z + 1, 4), lax.rem(z + 3, 4), lax.rem(z + 2, 4)
    dev_y = (jnp.where(core == 0, s, s_flip), fy)
    dev_up, dev_down = (s, 2 * up + y), (s, 2 * down + y)
    x_count = 4
    stride = count // x_count
    x_pos = s // stride
    along_x = [(lax.rem(s + k * stride, count), f) for k in range(1, x_count)]
    barrier = pltpu.get_barrier_semaphore()
    for peer in [dev_y, dev_up, dev_down, mate, beyond] + along_x:
        pl.semaphore_signal(barrier, inc=1, device_id=peer, device_id_type=MESH)
    pl.semaphore_wait(barrier, 5 + len(along_x))
    rows = wq_shard.shape[0]
    half = rows // 2
    quarter = rows // 4
    slice_rows = half // x_count
    arrays = ((wq_shard, wq), (wo_shard, wo))
    pending = []

    def start(copy):
        copy.start()
        return copy

    def part(owner, offset, size):
        return pl.ds(pl.multiple_of(owner * rows + core * half + offset, slice_rows), size)

    def send_to(a, k, owner, offset, size, peer, local):
        shard, full = arrays[a]
        place = part(owner, offset, size)
        source = shard.at[pl.ds(pl.multiple_of(core * half + offset, slice_rows), size)] if local else full.at[place]
        copy = start(pltpu.make_async_remote_copy(
            source, full.at[place], send.at[a, k], recv.at[a, k], device_id=peer, device_id_type=MESH))
        pending.append(copy)
        return copy

    def hand(a, k, owner):
        full = arrays[a][1]
        place = part(owner, 0, half)
        return start(pltpu.make_async_remote_copy(
            full.at[place], full.at[place], send2.at[a, k], recv2.at[a, k], device_id=mate, device_id_type=MESH))

    def send_y(a):
        return send_to(a, 0, f, x_pos * slice_rows, slice_rows, dev_y, True)

    def spread(a, first):
        first.wait_recv()
        return [send_to(a, 9 + k, fy, x_pos * slice_rows, slice_rows, peer, False) for k, peer in enumerate(along_x)]

    def send_own(a):
        return (send_to(a, 1, f, 0, half, dev_up, True), send_to(a, 2, f, 0, half, dev_down, True))

    def send_other(a):
        return (send_to(a, 3, fy, 0, half, dev_up, False), send_to(a, 4, fy, 0, half, dev_down, False))

    def onward(a, first, odd):
        lane = 1 - y if odd else y
        k = 7 if odd else 5
        h = 3 if odd else 1
        first[0].wait_recv()
        c_up = send_to(a, k, 2 * down + lane, 0, quarter, dev_up, False)
        h_up = hand(a, h, 2 * down + lane)
        first[1].wait_recv()
        c_down = send_to(a, k + 1, 2 * up + lane, quarter, quarter, dev_down, False)
        return (c_up, c_down), [h_up, hand(a, h + 1, 2 * up + lane)]

    def last(a, second, odd):
        second[0].wait_recv()
        second[1].wait_recv()
        return [hand(a, 6 if odd else 5, 2 * far + (1 - y if odd else y))]

    x_copy = start(pltpu.make_async_copy(x_hbm, x, own.at[2]))
    y_q = send_y(0)
    own_q = send_own(0)
    place = pl.ds(pl.multiple_of(f * rows, rows), rows)
    own_copy_q, own_copy_o = [
        start(pltpu.make_async_copy(shard, full.at[place], own.at[a])) for a, (shard, full) in enumerate(arrays)]
    y_o = send_y(1)
    inner_copy = start(pltpu.make_async_remote_copy(
        x_hbm, inner, x_send.at[8], x_recv.at[8], device_id=mate, device_id_type=MESH))
    spread_q = spread(0, y_q)
    step = x.shape[0] // 8
    outer_copies = []
    for i in range(8):
        place = pl.ds(i * step, step)
        outer_copies.append(start(pltpu.make_async_remote_copy(
            x_hbm.at[place], outer.at[place], x_send.at[i], x_recv.at[i], device_id=beyond, device_id_type=MESH)))
    for copy in spread_q:
        copy.wait_recv()
    other_q = send_other(0)
    hands_q = [hand(0, 0, fy)]
    spread_o = spread(1, y_o)
    onward_q, more = onward(0, own_q, False)
    hands_q += more
    onward_q2, more = onward(0, other_q, True)
    hands_q += more
    width = x.shape[1]
    tile = 512
    total = x.shape[0]
    blocks = total // BLOCK

    early = [pl.ds(pl.multiple_of(2 * pair * rows, 2 * rows), 2 * rows) for pair in (z, up, down)]
    late = pl.ds(pl.multiple_of(2 * far * rows, 2 * rows), 2 * rows)

    def begin(source, sums, offset, base=0):
        def one(n, _):
            w_cols = pl.ds(pl.multiple_of(offset + n * tile, tile), tile)
            s_cols = pl.ds(pl.multiple_of(offset - base + n * tile, tile), tile)
            terms = [
                jnp.dot(source[:, part_rows], wq[part_rows, w_cols], preferred_element_type=F32) for part_rows in early]
            sums[:, s_cols] = terms[0] + terms[1] + terms[2]
            return 0

        lax.fori_loop(0, width // tile, one, 0)

    def project(source, target, first, offset, sums=None, base=0):
        def one(n, _):
            w_cols = pl.ds(pl.multiple_of(offset + n * tile, tile), tile)
            if sums is None:
                value = jnp.dot(source[...], wq[:, w_cols], preferred_element_type=F32)
            else:
                s_cols = pl.ds(pl.multiple_of(offset - base + n * tile, tile), tile)
                value = sums[:, s_cols] + jnp.dot(source[:, late], wq[late, w_cols], preferred_element_type=F32)
            value = value.astype(BF16)
            cols = pl.ds(pl.multiple_of(n * tile, tile), tile)
            for j in range(value.shape[0] // BLOCK):
                piece = value[j * BLOCK:(j + 1) * BLOCK]
                if offset == 2 * width:
                    target[first + j, cols, :] = piece.T
                else:
                    target[first + j, :, cols] = piece
            return 0

        lax.fori_loop(0, width // tile, one, 0)

    x_copy.wait()
    own_copy_q.wait()
    for copy in hands_q:
        copy.wait_recv()
    for third in range(3):
        begin(x, own_sums, third * width)
    last_hands = last(0, onward_q, False) + last(0, onward_q2, True)
    hands_q += last_hands
    own_o = send_own(1)
    for copy in spread_o:
        copy.wait_recv()
    other_o = send_other(1)
    hands_o = [hand(1, 0, fy)]
    inner_copy.wait_recv()
    for third in (1, 2):
        begin(inner, inner_sums, third * width, width)
    for copy in last_hands:
        copy.wait_recv()
    project(x, q_sc, 0, 0, own_sums)
    project(x, k_sc, blocks, width, own_sums)
    onward_o, more = onward(1, own_o, False)
    hands_o += more
    project(x, vt_sc, blocks, 2 * width, own_sums)
    inner_first = (1 - core) * 2 * blocks
    project(inner, k_sc, inner_first, width, inner_sums, width)
    onward_o2, more = onward(1, other_o, True)
    hands_o += more
    project(inner, vt_sc, inner_first, 2 * width, inner_sums, width)
    hands_o += last(1, onward_o, False)
    hands_o += last(1, onward_o2, True)
    pieces = 2
    size = total // pieces
    for i in range(pieces):
        for copy in outer_copies[i * 8 // pieces:(i + 1) * 8 // pieces]:
            copy.wait_recv()
        piece = outer.at[pl.ds(i * size, size)]
        first = core * 2 * blocks + i * (size // BLOCK)
        project(piece, k_sc, first, width)
        project(piece, vt_sc, first, 2 * width)

    def step(scored, weighed):
        score_and_weigh(layout, counts, scored, weighed, q_sc, k_sc, vt_sc, (s0_sc, s1_sc), top_sc, att)

    pairs = HEADS // 2

    def block(b, _):
        for g in range(pairs):
            following = (b, g + 1) if g + 1 < pairs else (jnp.minimum(b + 1, blocks - 1), 0)
            step(following + ((g + 1) % 2,), (b, g, g % 2))
        return 0

    step((0, 0, 0), None)
    lax.fori_loop(0, blocks, block, 0)
    own_copy_o.wait()
    for copy in hands_o:
        copy.wait_recv()
    for c in range(0, width, tile):
        out[:, c:c + tile] = jnp.dot(att[...], wo[:, c:c + tile], preferred_element_type=F32).astype(BF16)
    for copy in pending + hands_q + hands_o + outer_copies + [inner_copy]:
        copy.wait_send()


def shards(normed, w_qkv, w_out, layout, counts):
    hbm = pl.BlockSpec(memory_space=pl.ANY)
    smem = pl.BlockSpec(memory_space=pltpu.SMEM)
    vmem = pl.BlockSpec(memory_space=pltpu.VMEM)
    dma = pltpu.SemaphoreType.DMA
    rows, width = normed.shape
    blocks = rows // BLOCK
    slots = layout.shape[1] + 1
    return pl.pallas_call(
        sublayer_kernel,
        out_shape=jax.ShapeDtypeStruct((rows, width), BF16),
        in_specs=[smem, smem, hbm, hbm, hbm],
        out_specs=vmem,
        scratch_shapes=[
            pltpu.VMEM((rows, width), BF16),
            pltpu.VMEM((8 * w_qkv.shape[0], w_qkv.shape[1]), BF16),
            pltpu.VMEM((8 * w_out.shape[0], w_out.shape[1]), BF16),
            pltpu.VMEM((rows, width), BF16),
            pltpu.VMEM((rows, width), BF16),
            pltpu.VMEM((blocks, BLOCK, width), BF16),
            pltpu.VMEM((3 * blocks, BLOCK, width), BF16),
            pltpu.VMEM((3 * blocks, width, BLOCK), BF16),
            pltpu.VMEM((slots, BLOCK, 2 * HEAD), F32),
            pltpu.VMEM((slots, BLOCK, 2 * HEAD), F32),
            pltpu.VMEM((2, 8, 2 * HEAD), F32),
            pltpu.VMEM((rows, width), BF16),
            pltpu.VMEM((rows, 3 * width), F32),
            pltpu.VMEM((rows, 2 * width), F32),
            dma((2, 12)), dma((2, 12)), dma((2, 7)), dma((2, 7)), dma((3,)), dma((9,)), dma((9,)),
        ],
        compiler_params=pltpu.CompilerParams(
            collective_id=0, has_side_effects=True, vmem_limit_bytes=60 << 20),
        name="sublayer",
    )(layout, counts, normed, w_qkv, w_out)


def solution(mesh):
    return jax.shard_map(
        shards,
        mesh=mesh,
        in_specs=(
            P(("seq", "fsdp"), None),
            P("fsdp", None),
            P("fsdp", None),
            P(("seq", "fsdp"), None),
            P(("seq", "fsdp")),
        ),
        out_specs=P(("seq", "fsdp"), None),
        check_vma=False,
    )
```
